128 devices in a mesh: sky: 16 (over y, x), tm: 4 (over z), fov: 2 (over core).
Axes of the slice: x: 4, y: 4, z: 4, core: 2. Of those that a mesh axis runs over, the one named last changes fastest.
Arguments:
- src_partials: float32 [262144, 5, 128], P(('sky', 'tm', 'fov')), may hold values from -0.375 to 0.375
- att_partials: float32 [262144, 4, 128], P(('sky', 'tm', 'fov')), may hold values from -0.3 to 0.3
- cal_partials: float32 [262144, 128], P(('sky', 'tm', 'fov')), may hold values from -0.6 to 0.6
- obs_phase: float32 [262144, 128], P(('sky', 'tm', 'fov')), may hold values from 0 to 1
- obs_residual: float32 [262144, 128], P(('sky', 'tm', 'fov')), may hold values from -6 to 6
- block_source: int32 [262144], P(('sky', 'tm', 'fov')), may hold values from 0 to 4095
- block_segment: int32 [262144], P(('sky', 'tm', 'fov')), may hold values from 0 to 2047, as said below
- block_unit: int32 [262144], P(('sky', 'tm', 'fov')), may hold values from 0 to 524287, as said below
- live_blocks: int32 [128], P(('sky', 'tm', 'fov')), may hold values from 608 to 2048, as said below
Outputs:
- src_update: float32 [5, 65536], P(None, 'sky')
- att_update: float32 [4, 4, 2048], P(None, 'tm', 'sky')
- cal_update: float32 [524288], P(('sky', 'tm', 'fov'))
The draws below stay inside these ranges and needn't reach their ends.
Inputs may be any that keep to these rules, and one draw needn't show every extreme that they name: `block_segment`: only live blocks' segments matter. Of one device's live blocks at most 128 have segments of one sky index (s * 128 to (s + 1) * 128 - 1); for every tm and fov index some sky index s has exactly 128 such live blocks from every device of that tm and fov index. A device's live blocks are its first live_blocks blocks. `block_unit`: units fall into 128 ranges of 524288 / 128 units each (range r is the units of output shard r). Of one device's blocks, live or not, at most 32 have units of one range; on every device some range has exactly 32.
All inputs are finite; a program needn't handle non-finite values.
Results may differ from the reference program's by a relative error of at most 0.00011.
Values sent between devices are 32-bit elements; how exact they have to be, the bound alone decides.
No kernel may reach another device: no remote copies, remote signals or barrier semaphores. Data moves between devices by JAX's collectives and lax.ppermute only.
A program may use at most 128 MiB of HBM per device.

```python
import jax
import jax.numpy as jnp
from jax import lax

SRC_DEV = 4096
BLK_DEV = 2048
SEG_DEV = 128
OBS = 128
CAL = 524288
SRC = 65536
BLOCKS = 262144
SEG_ARC = 2048
N_SKY = 16
N_TM = 4
N_FOV = 2


def block_layout(key):
    key = jax.random.fold_in(key, 7)
    key_count, key_hot, key_segment, key_order = jax.random.split(key, 4)
    capacity = BLK_DEV // N_SKY
    device_total = N_SKY * N_TM * N_FOV
    counts = jax.random.randint(key_count, (N_SKY, N_TM, N_FOV, N_SKY), capacity // 4, capacity + 1)
    hottest = jax.random.randint(key_hot, (1, N_TM, N_FOV, 1), 0, N_SKY)
    column = jnp.arange(N_SKY).reshape(1, 1, 1, N_SKY)
    counts = jnp.where(column == hottest, capacity, counts)
    counts = counts.at[0, 0, 0, :].set(capacity)
    lowest = jnp.where(jnp.arange(N_SKY) == hottest[0, N_TM - 1, N_FOV - 1, 0], capacity, capacity // 4)
    counts = counts.at[N_SKY - 1, N_TM - 1, N_FOV - 1, :].set(lowest)
    counts = counts.reshape(device_total, N_SKY)
    slots = jnp.arange(BLK_DEV, dtype=jnp.int32)
    target = slots // capacity
    ranks = slots % capacity
    live_slot = (ranks[None, :] < jnp.take(counts, target, axis=1)).astype(jnp.int32)
    within = jax.random.randint(key_segment, (device_total, BLK_DEV), 0, SEG_DEV)
    segment = target[None, :] * SEG_DEV + within
    scores = jax.random.randint(key_order, (device_total, BLK_DEV), 0, BLK_DEV) * BLK_DEV + slots[None, :]
    first = jnp.argsort(scores, axis=1)
    live_sorted = jnp.take_along_axis(live_slot, first, axis=1)
    second = jnp.argsort(1 - live_sorted, axis=1, stable=True)
    order = jnp.take_along_axis(first, second, axis=1)
    segment = jnp.take_along_axis(segment, order, axis=1).reshape(-1)
    totals = jnp.sum(live_slot, axis=1)
    return (segment.astype(jnp.int32), totals.astype(jnp.int32))


def draw_block_segment(key, part):
    return block_layout(key)[0]


def draw_live_blocks(key, part):
    return block_layout(key)[1]


def unit_row(key):
    key_hot, key_order, key_shuffle, key_unit = jax.random.split(key, 4)
    owners = N_SKY * N_TM * N_FOV
    ucap = max(2, 2 * BLK_DEV // owners)
    share = CAL // owners
    slot_total = owners * ucap
    slots = jnp.arange(slot_total, dtype=jnp.int32)
    hot = jax.random.randint(key_hot, (), 0, owners)
    scores = jax.random.randint(key_order, (slot_total,), 0, slot_total) * slot_total + slots
    scores = jnp.where(slots // ucap == hot, slots - slot_total, scores)
    chosen = jnp.argsort(scores)[:BLK_DEV]
    chosen = jax.random.permutation(key_shuffle, chosen)
    owner = chosen // ucap
    inner = jax.random.randint(key_unit, (BLK_DEV,), 0, share)
    return (owner * share + inner).astype(jnp.int32)


def draw_block_unit(key, part):
    key = jax.random.fold_in(key, 11)
    keys = jax.random.split(key, N_SKY * N_TM * N_FOV)
    return jax.vmap(unit_row)(keys).reshape(-1)


def plant(values, stream_key, low, high):
    longest = values.shape.index(max(values.shape))
    spots = []
    for shift in (0, 1):
        where = [jax.random.randint(jax.random.fold_in(stream_key, axis), (), 0, length) for axis, length in enumerate(values.shape)]
        where[longest] = (where[longest] + shift) % values.shape[longest]
        spots.append(tuple(where))
    return values.at[spots[0]].set(low).at[spots[1]].set(high)


def level_of(own_key, shape, shards, smallest, high):
    level = 1.0
    for axis_at, shards_of in shards:
        heights = jax.random.uniform(jax.random.fold_in(jax.random.fold_in(own_key, 6), axis_at), (shards_of,), jnp.float32, smallest / len(shards), high / len(shards))
        level = level * jnp.repeat(jnp.exp(heights), shape[axis_at] // shards_of).reshape((-1,) + (1,) * (len(shape) - 1 - axis_at))
    return level


def gaussian(stream_key, shape, spread, reach, cuts=(), kind=jnp.bfloat16):
    array = jax.random.normal(stream_key, shape, jnp.float32) * spread
    if len(cuts) > 0:
        array = level_of(stream_key, shape, cuts, -0.22, 0.18) * array
    return jnp.clip(array, min=-reach, max=reach).astype(kind)


def setup_inputs(seed: int = 0) -> dict:
    streams_of = jax.random.split(jax.random.key(seed), 10)
    return {
        "src_partials": gaussian(streams_of[0], (BLOCKS, 5, OBS), 0.0625, 0.375, ((0, 128),), jnp.float32),
        "att_partials": gaussian(streams_of[1], (BLOCKS, 4, OBS), 0.05, 0.3, ((0, 128),), jnp.float32),
        "cal_partials": gaussian(streams_of[2], (BLOCKS, OBS), 0.1, 0.6, ((0, 128),), jnp.float32),
        "obs_phase": jnp.clip(1.0 * jax.random.uniform(streams_of[3], (BLOCKS, OBS), jnp.float32) ** level_of(streams_of[3], (BLOCKS, OBS), ((0, 128),), -0.2, 0.2), 0.0, 1.0),
        "obs_residual": gaussian(streams_of[4], (BLOCKS, OBS), 1.0, 6.0, ((0, 128),), jnp.float32),
        "block_source": plant(jax.random.randint(streams_of[5], (BLOCKS,), 0, SRC_DEV), jax.random.fold_in(streams_of[5], 1), 0, SRC_DEV - 1).astype(jnp.int32),
        "block_segment": draw_block_segment(jax.random.fold_in(streams_of[9], 71), 0),
        "block_unit": draw_block_unit(jax.random.fold_in(streams_of[9], 71), 0),
        "live_blocks": draw_live_blocks(jax.random.fold_in(streams_of[9], 71), 0),
    }


index_pairs = [(i, j) for i in range(5) for j in range(i, 5)]

def spline_basis(phase):
    rest = 1.0 - phase
    square = phase * phase
    cubed = square * phase
    return jnp.stack([rest * rest * rest / 6.0, (3.0 * cubed - 6.0 * square + 4.0) / 6.0, (-3.0 * cubed + 3.0 * square + 3.0 * phase + 1.0) / 6.0, cubed / 6.0], axis=1)

def spline_products(residual, partials, phase):
    basis = spline_basis(phase)
    weighted = partials * residual[:, None, :]
    right_side = jnp.einsum('bjo,bco->bjc', basis, weighted, precision=lax.Precision.HIGHEST)
    diag_part = jnp.einsum('bjo,bco->bjc', basis * basis, partials * partials, precision=lax.Precision.HIGHEST)
    return jnp.concatenate([right_side, diag_part], axis=2)

def block_products(partials, residual, live_mask):
    products = jnp.stack([lax.optimization_barrier(jnp.sum(partials[:, i, :] * partials[:, j, :], axis=1)) for i, j in index_pairs], axis=1)
    right_side = lax.optimization_barrier(jnp.sum(partials * residual[:, None, :], axis=2))
    return (products * live_mask[:, None], right_side * live_mask[:, None])

def solve_normals(packed, right_side):
    matrix = {}
    for position, (i, j) in enumerate(index_pairs):
        matrix[i, j] = packed[position] + (1.0 if i == j else 0.0)
    factor = {}
    for i in range(5):
        for j in range(i + 1):
            running = matrix[j, i]
            for k in range(j):
                running = running - factor[i, k] * factor[j, k]
            if i == j:
                factor[i, i] = jnp.sqrt(running)
            else:
                factor[i, j] = running / factor[j, j]
    forward = []
    for i in range(5):
        running = right_side[i]
        for k in range(i):
            running = running - factor[i, k] * forward[k]
        forward.append(running / factor[i, i])
    result = [forward[0]] * 5
    for i in reversed(range(5)):
        running = forward[i]
        for k in range(i + 1, 5):
            running = running - factor[k, i] * result[k]
        result[i] = running / factor[i, i]
    return jnp.stack(result)

def reference(src_partials, att_partials, cal_partials, obs_phase, obs_residual, block_source, block_segment, block_unit, live_blocks):
    block_count = src_partials.shape[0]
    position = jnp.arange(block_count, dtype=jnp.int32)
    device_of = (position // BLK_DEV).astype(jnp.int32)
    live_mask = (position % BLK_DEV < live_blocks[device_of]).astype(jnp.float32)
    sky_of = device_of // (N_TM * N_FOV)
    arc_of = device_of // N_FOV % N_TM
    source_global = (sky_of * SRC_DEV + block_source).astype(jnp.int32)
    products, right_side = block_products(src_partials, obs_residual, live_mask)
    normals = jax.ops.segment_sum(products, source_global, num_segments=SRC).T
    source_right = jax.ops.segment_sum(right_side, source_global, num_segments=SRC).T
    src_update = solve_normals(normals, source_right)
    chosen = src_update[:, source_global].T
    residual = obs_residual - lax.optimization_barrier(jnp.sum(src_partials * chosen[:, :, None], axis=1))
    values = spline_products(residual, att_partials, obs_phase) * live_mask[:, None, None]
    offsets = block_segment[:, None] + jnp.arange(4, dtype=jnp.int32)[None, :]
    knot_total = N_TM * SEG_ARC
    knot_index = jnp.where(offsets < SEG_ARC, arc_of[:, None] * SEG_ARC + offsets, knot_total).astype(jnp.int32)
    knots = jax.ops.segment_sum(values.reshape(-1, 8), knot_index.reshape(-1), num_segments=knot_total + 1)[:knot_total]
    attitude = knots[:, :4] / (1.0 + knots[:, 4:])
    att_update = attitude.T.reshape(4, N_TM, SEG_ARC)
    unit_right = jax.ops.segment_sum(lax.optimization_barrier(jnp.sum(cal_partials * residual, axis=1)) * live_mask, block_unit, num_segments=CAL)
    unit_diag = jax.ops.segment_sum(lax.optimization_barrier(jnp.sum(cal_partials * cal_partials, axis=1)) * live_mask, block_unit, num_segments=CAL)
    cal_update = unit_right / (1.0 + unit_diag)
    return (src_update, att_update, cal_update)
```

```python
import jax
import jax.numpy as jnp
from jax import lax
from jax.experimental import pallas as pl
from jax.experimental.pallas import tpu as pltpu
from jax.sharding import PartitionSpec as P

BLK = 2048
NB = 256
STEPS = BLK // NB
OBS = 128
CAP = 32
RANGES = 128
SHARE = 4096
PIECES = 9
F32 = jnp.float32
BF16 = jnp.bfloat16
ALL = ("sky", "tm", "fov")

index_pairs = [(i, j) for i in range(5) for j in range(i, 5)]


def split_parts(x, count):
    parts = []
    for _ in range(count - 1):
        part = x.astype(BF16)
        parts.append(part)
        x = x - part.astype(F32)
    parts.append(x.astype(BF16))
    return parts


def dot_nt(a, b):
    return lax.dot_general(a, b, (((1,), (1,)), ((), ())), preferred_element_type=F32)


def dot_nn(a, b):
    return lax.dot_general(a, b, (((1,), (0,)), ((), ())), preferred_element_type=F32)


def rows_equal(count, row, dtype=F32):
    iota = lax.broadcasted_iota(jnp.int32, (count, row.shape[1]), 0)
    return jnp.where(iota == row, 1.0, 0.0).astype(dtype)


def accumulate(ref, product, step):
    @pl.when(step == 0)
    def _():
        ref[...] = product

    @pl.when(step > 0)
    def _():
        ref[...] += product


def live_row(info_ref, step):
    position = step * NB + lax.broadcasted_iota(jnp.int32, (1, NB), 1)
    return jnp.where(position < info_ref[0], 1.0, 0.0)


def column_sum(x):
    return jnp.sum(x, axis=0, keepdims=True)


def spline_basis(phase):
    rest = 1.0 - phase
    square = phase * phase
    cubed = square * phase
    half = 0.5 * cubed
    return (
        rest * rest * rest * (1.0 / 6.0),
        half - square + (2.0 / 3.0),
        0.5 * (square + phase) - half + (1.0 / 6.0),
        cubed * (1.0 / 6.0),
    )


def normals_kernel(info_ref, src_ref, res_ref, idx_ref, keep_ref, send_ref, srct_ref, acc_ref):
    step = pl.program_id(0)
    for i in range(5):
        srct_ref[i] = src_ref[i].T
    srct_ref[5] = res_ref[...].T
    idx = idx_ref[0] ^ (info_ref[1] * 2048)
    high = rows_equal(16, idx >> 8) * live_row(info_ref, step)
    low = rows_equal(256, idx & 255, BF16)
    halves = []
    for h in range(NB // 128):
        lanes = slice(h * 128, (h + 1) * 128)
        sums = [None] * 20
        for o in range(OBS // 8):
            rows = [srct_ref[i, o * 8 : o * 8 + 8, lanes] for i in range(6)]
            terms = [rows[i] * rows[j] for i, j in index_pairs] + [rows[i] * rows[5] for i in range(5)]
            sums = terms if o == 0 else [s + t for s, t in zip(sums, terms)]
        halves.append([column_sum(s) for s in sums])
    pieces = []
    for k in range(20):
        row = jnp.concatenate([half[k] for half in halves], axis=1)
        pieces.append(high * row)
    stacked = jnp.concatenate(pieces, axis=0)
    left = jnp.concatenate(split_parts(stacked, 3), axis=0)
    accumulate(acc_ref, dot_nt(left, low), step)

    @pl.when(step == STEPS - 1)
    def _():
        for k in range(20):
            total = (
                acc_ref[k * 16 : k * 16 + 16]
                + acc_ref[320 + k * 16 : 320 + k * 16 + 16]
                + acc_ref[640 + k * 16 : 640 + k * 16 + 16]
            )
            keep_ref[k] = total[:8]
            send_ref[k] = total[8:]


def shifted(rows, distance):
    if distance == 0:
        return rows
    moved = pltpu.roll(rows, distance, 1)
    below = pltpu.roll(moved, 1, 0)
    row = lax.broadcasted_iota(jnp.int32, rows.shape, 0)
    lane = lax.broadcasted_iota(jnp.int32, rows.shape, 1)
    return jnp.where(lane >= distance, moved, jnp.where(row > 0, below, 0.0))


def knots_of(acc_ref, c):
    total = None
    for j in range(4):
        start = (j * 4 + c) * 8
        part = acc_ref[start : start + 8] + acc_ref[128 + start : 128 + start + 8]
        part = shifted(part, j)
        total = part if total is None else total + part
    return total


def diag_kernel(
    info_ref, att_ref, pha_ref, cal_ref, seg_ref, unit_ref,
    extra_ref, rank_ref, knots_ref, slots_ref, acc_ref, slot_ref, carry_ref,
):
    step = pl.program_id(0)
    live = live_row(info_ref, step)
    for c in range(4):
        for h in range(NB // 128):
            rows = att_ref[pl.ds(h * 512 + c, 128, stride=4), :]
            extra_ref[c, :, h * 128 : (h + 1) * 128] = rows.T
    extra_ref[4] = pha_ref[...].T
    extra_ref[5] = cal_ref[...].T
    seg = seg_ref[0]
    seg_high = rows_equal(8, seg >> 8) * live
    seg_low = rows_equal(256, seg & 255, BF16)
    halves = []
    for h in range(NB // 128):
        lanes = slice(h * 128, (h + 1) * 128)
        sums = [None] * 17
        for o in range(OBS // 8):
            rows = [extra_ref[i, o * 8 : o * 8 + 8, lanes] for i in range(6)]
            basis = [b * b for b in spline_basis(rows[4])]
            squares = [rows[c] * rows[c] for c in range(4)]
            terms = [b * s for b in basis for s in squares] + [rows[5] * rows[5]]
            sums = terms if o == 0 else [s + t for s, t in zip(sums, terms)]
        halves.append([column_sum(s) for s in sums])
    sums = [jnp.concatenate([half[k] for half in halves], axis=1) for k in range(17)]
    stacked = jnp.concatenate([seg_high * sums[k] for k in range(16)], axis=0)
    accumulate(acc_ref, dot_nt(jnp.concatenate(split_parts(stacked, 2), axis=0), seg_low), step)

    unit = unit_ref[0]
    owner = rows_equal(RANGES, unit >> 12)
    owner_low = owner.astype(BF16)
    before = lax.broadcasted_iota(jnp.int32, (NB, NB), 0) < lax.broadcasted_iota(jnp.int32, (NB, NB), 1)
    before = jnp.where(before, 1.0, 0.0).astype(BF16)
    earlier = dot_nn(owner_low, before) + jnp.where(step > 0, carry_ref[...], 0.0)
    rank = column_sum(owner * earlier)
    accumulate(carry_ref, dot_nn(owner_low, jnp.ones((NB, NB), BF16)), step)
    rank = rank.astype(jnp.int32)
    rank_ref[0] = rank
    place = rows_equal(CAP, rank)
    inner = (unit & (SHARE - 1)).astype(F32)
    stacked = jnp.concatenate([place * (sums[16] * live), place * inner], axis=0)
    accumulate(slot_ref, dot_nt(jnp.concatenate(split_parts(stacked, 2), axis=0), owner_low), step)

    @pl.when(step == STEPS - 1)
    def _():
        for c in range(4):
            knots_ref[c] = knots_of(acc_ref, c)
        slots_ref[...] = slot_ref[:64] + slot_ref[64:]


def solve_kernel(a_ref, b_ref, c_ref, d_ref, out_ref):
    packed = [(a_ref[k] + c_ref[k]) + (b_ref[k] + d_ref[k]) for k in range(20)]
    matrix = {}
    for position, (i, j) in enumerate(index_pairs):
        matrix[i, j] = packed[position] + (1.0 if i == j else 0.0)
    factor = {}
    inverse = {}
    for i in range(5):
        for j in range(i + 1):
            running = matrix[j, i]
            for k in range(j):
                running = running - factor[i, k] * factor[j, k]
            if i == j:
                inverse[i] = 1.0 / jnp.sqrt(running)
            else:
                factor[i, j] = running * inverse[j]
    forward = []
    for i in range(5):
        running = packed[15 + i]
        for k in range(i):
            running = running - factor[i, k] * forward[k]
        forward.append(running * inverse[i])
    result = [None] * 5
    for i in reversed(range(5)):
        running = forward[i]
        for k in range(i + 1, 5):
            running = running - factor[k, i] * result[k]
        result[i] = running * inverse[i]
        out_ref[i] = result[i]


def apply_kernel(
    info_ref, srct_ref, extra_ref, idx_ref, seg_ref, unit_ref, rank_ref, mine_ref, other_ref,
    diag_ref, slots_ref, out_ref, update_ref, table_ref, acc_ref, slot_ref,
):
    step = pl.program_id(0)
    fov = info_ref[1]

    @pl.when(step == 0)
    def _():
        out_ref[...] = jnp.zeros_like(out_ref)
        pieces = []
        for k in range(5):
            mine = mine_ref[k]
            other = other_ref[k]
            pieces += [mine, other]
            first = jnp.where(fov == 0, mine, other)
            second = jnp.where(fov == 0, other, mine)
            for q in range(8):
                update_ref[k : k + 1, q * 256 : (q + 1) * 256] = first[q : q + 1]
                update_ref[k : k + 1, 2048 + q * 256 : 2048 + (q + 1) * 256] = second[q : q + 1]
        stacked = jnp.concatenate(pieces, axis=0)
        table_ref[...] = jnp.concatenate(split_parts(stacked, 3), axis=0)

    live = live_row(info_ref, step)
    idx = idx_ref[0] ^ (fov * 2048)
    high = rows_equal(16, idx >> 8)
    low = rows_equal(256, idx & 255, BF16)
    looked = dot_nn(table_ref[...], low)
    looked = looked[:80] + looked[80:160] + looked[160:240]
    chosen = [column_sum(looked[k * 16 : k * 16 + 16] * high) for k in range(5)]
    halves = []
    for h in range(NB // 128):
        lanes = slice(h * 128, (h + 1) * 128)
        spread = [jnp.broadcast_to(chosen[k][:, lanes], (8, 128)) for k in range(5)]
        sums = [None] * 17
        for o in range(OBS // 8):
            span = slice(o * 8, o * 8 + 8)
            model = srct_ref[0, span, lanes] * spread[0]
            for k in range(1, 5):
                model = model + srct_ref[k, span, lanes] * spread[k]
            residual = srct_ref[5, span, lanes] - model
            basis = spline_basis(extra_ref[4, span, lanes])
            weighted = [extra_ref[c, span, lanes] * residual for c in range(4)]
            terms = [b * w for b in basis for w in weighted] + [extra_ref[5, span, lanes] * residual]
            sums = terms if o == 0 else [s + t for s, t in zip(sums, terms)]
        halves.append([column_sum(s) for s in sums])
    sums = [jnp.concatenate([half[k] for half in halves], axis=1) for k in range(17)]
    seg = seg_ref[0]
    seg_high = rows_equal(8, seg >> 8) * live
    seg_low = rows_equal(256, seg & 255, BF16)
    stacked = jnp.concatenate([seg_high * sums[k] for k in range(16)], axis=0)
    accumulate(acc_ref, dot_nt(jnp.concatenate(split_parts(stacked, 2), axis=0), seg_low), step)
    owner = rows_equal(RANGES, unit_ref[0] >> 12, BF16)
    placed = rows_equal(CAP, rank_ref[0]) * (sums[16] * live)
    accumulate(slot_ref, dot_nt(jnp.concatenate(split_parts(placed, 2), axis=0), owner), step)

    @pl.when(step == STEPS - 1)
    def _():
        tm = info_ref[2]
        slots = jnp.concatenate(
            [slot_ref[:CAP] + slot_ref[CAP:], slots_ref[...], jnp.zeros((CAP, RANGES), F32)], axis=0
        )
        out_ref[pl.ds(0, RANGES, stride=PIECES), :] = slots.T
        for c in range(8):
            knots = knots_of(acc_ref, c) if c < 4 else diag_ref[c - 4]
            for r in range(2):
                for f in range(2):
                    start = r * 8 * PIECES + (tm * 2 + f) * PIECES + 1 + c
                    out_ref[pl.ds(start, 8, stride=16 * PIECES), :] = knots[:, r * 128 : (r + 1) * 128]


def final_kernel(info_ref, in_ref, att_ref, cal_ref, left_ref, right_ref):
    tm = info_ref[2]
    knots = None
    for s in range(16):
        for f in range(2):
            part = in_ref[pl.ds((s * 8 + tm * 2 + f) * PIECES + 1, 8), :]
            knots = part if knots is None else knots + part
    att_ref[...] = knots[:4] / (1.0 + knots[4:])
    slots = in_ref[pl.ds(0, RANGES, stride=PIECES), :].T
    unit = slots[64:96].astype(jnp.int32)
    for k in range(CAP):
        lanes = slice(k * 128, (k + 1) * 128)
        inner = unit[k : k + 1]
        right_ref[:, lanes] = rows_equal(128, inner & 127, BF16)
        high = rows_equal(32, inner >> 7)
        stacked = jnp.concatenate([high * slots[k : k + 1], high * slots[32 + k : 33 + k]], axis=0)
        left_ref[:, lanes] = jnp.concatenate(split_parts(stacked, 2), axis=0)
    sums = dot_nt(left_ref[...], right_ref[...])
    sums = sums[:64] + sums[64:]
    cal_ref[...] = sums[:32] / (1.0 + sums[32:])


SMEM = pl.BlockSpec(memory_space=pltpu.SMEM)
ROW = pl.BlockSpec((1, 1, NB), lambda s: (s, 0, 0))


def whole(shape):
    return pl.BlockSpec(shape, lambda s: (0,) * len(shape))


def shards(
    src_partials,
    att_partials,
    cal_partials,
    obs_phase,
    obs_residual,
    block_source,
    block_segment,
    block_unit,
    live_blocks,
):
    tm = lax.axis_index("tm")
    fov = lax.axis_index("fov")
    info = jnp.stack([live_blocks[0], fov.astype(jnp.int32), tm.astype(jnp.int32)])
    source = block_source.reshape(STEPS, 1, NB)
    segment = block_segment.reshape(STEPS, 1, NB)
    unit = block_unit.reshape(STEPS, 1, NB)
    src = jnp.transpose(src_partials, (1, 0, 2))
    att = att_partials.reshape(BLK * 4, OBS)
    sequential = pltpu.CompilerParams(dimension_semantics=("arbitrary",))
    keep, send, srct = pl.pallas_call(
        normals_kernel,
        grid=(STEPS,),
        in_specs=[
            SMEM,
            pl.BlockSpec((5, NB, OBS), lambda s: (0, s, 0)),
            pl.BlockSpec((NB, OBS), lambda s: (s, 0)),
            ROW,
        ],
        out_specs=[
            whole((20, 8, 256)),
            whole((20, 8, 256)),
            pl.BlockSpec((6, OBS, NB), lambda s: (0, 0, s)),
        ],
        out_shape=[
            jax.ShapeDtypeStruct((20, 8, 256), F32),
            jax.ShapeDtypeStruct((20, 8, 256), F32),
            jax.ShapeDtypeStruct((6, OBS, BLK), F32),
        ],
        scratch_shapes=[pltpu.VMEM((960, 256), F32)],
        compiler_params=sequential,
        name="normals",
    )(info, src, obs_residual, source)
    half = keep + lax.ppermute(send, "fov", [(0, 1), (1, 0)])
    half, info_later = lax.optimization_barrier((half, info))
    around = [lax.ppermute(half, "tm", [(i, (i + d) % 4) for i in range(4)]) for d in (1, 2, 3)]
    extra, rank, diag_knots, diag_slots = pl.pallas_call(
        diag_kernel,
        grid=(STEPS,),
        in_specs=[
            SMEM,
            pl.BlockSpec((NB * 4, OBS), lambda s: (s, 0)),
            pl.BlockSpec((NB, OBS), lambda s: (s, 0)),
            pl.BlockSpec((NB, OBS), lambda s: (s, 0)),
            ROW,
            ROW,
        ],
        out_specs=[
            pl.BlockSpec((6, OBS, NB), lambda s: (0, 0, s)),
            ROW,
            whole((4, 8, 256)),
            whole((64, RANGES)),
        ],
        out_shape=[
            jax.ShapeDtypeStruct((6, OBS, BLK), F32),
            jax.ShapeDtypeStruct((STEPS, 1, NB), jnp.int32),
            jax.ShapeDtypeStruct((4, 8, 256), F32),
            jax.ShapeDtypeStruct((64, RANGES), F32),
        ],
        scratch_shapes=[
            pltpu.VMEM((256, 256), F32),
            pltpu.VMEM((128, RANGES), F32),
            pltpu.VMEM((RANGES, NB), F32),
        ],
        compiler_params=sequential,
        cost_estimate=pl.CostEstimate(flops=200_000_000, bytes_accessed=12_000_000, transcendentals=0),
        name="diag",
    )(info_later, att, obs_phase, cal_partials, segment, unit)
    around, diag_knots = lax.optimization_barrier((around, diag_knots))
    mine = pl.pallas_call(
        solve_kernel,
        out_shape=jax.ShapeDtypeStruct((5, 8, 256), F32),
        name="solve",
    )(half, *around)
    other = lax.ppermute(mine, "fov", [(0, 1), (1, 0)])
    outgoing, src_update = pl.pallas_call(
        apply_kernel,
        grid=(STEPS,),
        in_specs=[
            SMEM,
            pl.BlockSpec((6, OBS, NB), lambda s: (0, 0, s)),
            pl.BlockSpec((6, OBS, NB), lambda s: (0, 0, s)),
            ROW,
            ROW,
            ROW,
            ROW,
            whole((5, 8, 256)),
            whole((5, 8, 256)),
            whole((4, 8, 256)),
            whole((64, RANGES)),
        ],
        out_specs=[whole((128 * PIECES, 128)), whole((5, 4096))],
        out_shape=[
            jax.ShapeDtypeStruct((128 * PIECES, 128), F32),
            jax.ShapeDtypeStruct((5, 4096), F32),
        ],
        scratch_shapes=[
            pltpu.VMEM((240, 256), BF16),
            pltpu.VMEM((256, 256), F32),
            pltpu.VMEM((64, RANGES), F32),
        ],
        compiler_params=sequential,
        name="apply",
    )(info, srct, extra, source, segment, unit, rank, mine, other, diag_knots, diag_slots)
    arrived = lax.all_to_all(
        outgoing.reshape(128, 1, PIECES * 128), ALL, split_axis=0, concat_axis=0, tiled=True
    ).reshape(128 * PIECES, 128)
    att_update, cal_update = pl.pallas_call(
        final_kernel,
        in_specs=[SMEM, pl.BlockSpec(memory_space=pltpu.VMEM)],
        out_shape=[
            jax.ShapeDtypeStruct((4, 128), F32),
            jax.ShapeDtypeStruct((32, 128), F32),
        ],
        scratch_shapes=[pltpu.VMEM((128, CAP * 128), BF16), pltpu.VMEM((128, CAP * 128), BF16)],
        name="final",
    )(info, arrived)
    return (src_update, att_update.reshape(4, 1, 128), cal_update.reshape(SHARE))


def solution(mesh):
    return jax.shard_map(
        shards,
        mesh=mesh,
        in_specs=(
            P(ALL, None, None),
            P(ALL, None, None),
            P(ALL, None),
            P(ALL, None),
            P(ALL, None),
            P(ALL),
            P(ALL),
            P(ALL),
            P(ALL),
        ),
        out_specs=(P(None, "sky"), P(None, "tm", "sky"), P(ALL)),
        check_vma=False,
    )
```

```python
import jax
import jax.numpy as jnp
from jax import lax
from jax.experimental import pallas as pl
from jax.experimental.pallas import tpu as pltpu
from jax.sharding import PartitionSpec as P

BLK = 2048
NB = 256
STEPS = BLK // NB
OBS = 128
CAP = 32
RANGES = 128
SHARE = 4096
PIECES = 5
F32 = jnp.float32
BF16 = jnp.bfloat16
ALL = ("sky", "tm", "fov")

index_pairs = [(i, j) for i in range(5) for j in range(i, 5)]


def split_parts(x, count):
    parts = []
    for _ in range(count - 1):
        part = x.astype(BF16)
        parts.append(part)
        x = x - part.astype(F32)
    parts.append(x.astype(BF16))
    return parts


def dot_nt(a, b):
    return lax.dot_general(a, b, (((1,), (1,)), ((), ())), preferred_element_type=F32)


def dot_nn(a, b):
    return lax.dot_general(a, b, (((1,), (0,)), ((), ())), preferred_element_type=F32)


def packed_dot(left, right, count):
    return dot_nt(
        jnp.concatenate(split_parts(left, count), axis=1), jnp.concatenate([right] * count, axis=1)
    )


def rows_equal(count, row):
    iota = lax.broadcasted_iota(jnp.int32, (count, row.shape[1]), 0)
    return jnp.where(iota == row, 1.0, 0.0)


def narrow_rows_equal(count, row):
    iota = lax.broadcasted_iota(jnp.int32, (count, row.shape[1]), 0).astype(F32).astype(BF16)
    wide = jnp.broadcast_to(row.astype(F32), (count, row.shape[1])).astype(BF16)
    return jnp.where(iota == wide, jnp.ones((), BF16), jnp.zeros((), BF16))


def accumulate(ref, product, step):
    @pl.when(step == 0)
    def _():
        ref[...] = product

    @pl.when(step > 0)
    def _():
        ref[...] += product


def live_row(live_ref, step):
    position = step * NB + lax.broadcasted_iota(jnp.int32, (1, NB), 1)
    return jnp.where(position < live_ref[0], 1.0, 0.0)


def column_sum(x):
    return jnp.sum(x, axis=0, keepdims=True)


def spline_basis(phase):
    rest = 1.0 - phase
    square = phase * phase
    cubed = square * phase
    half = 0.5 * cubed
    return (
        rest * rest * rest * (1.0 / 6.0),
        half - square + (2.0 / 3.0),
        0.5 * (square + phase) - half + (1.0 / 6.0),
        cubed * (1.0 / 6.0),
    )


def spline_from_moments(m, j):
    sixth = 1.0 / 6.0
    if j == 0:
        return (m[0] - m[3]) * sixth + 0.5 * (m[2] - m[1])
    if j == 1:
        return m[0] * (2.0 / 3.0) - m[2] + 0.5 * m[3]
    if j == 2:
        return m[0] * sixth + 0.5 * (m[1] + m[2] - m[3])
    return m[3] * sixth


def normals_kernel(live_ref, src_ref, res_ref, idx_ref, keep_ref, send_ref, srct_ref, acc_ref):
    step = pl.program_id(0)
    for i in range(5):
        srct_ref[i] = src_ref[i].T
    srct_ref[5] = res_ref[...].T
    idx = idx_ref[0] ^ (lax.axis_index("fov") * 2048)
    high = rows_equal(16, idx >> 8) * live_row(live_ref, step)
    low = narrow_rows_equal(256, idx & 255)
    halves = []
    for h in range(NB // 128):
        lanes = slice(h * 128, (h + 1) * 128)
        sums = [None] * 20
        for o in range(OBS // 8):
            rows = [srct_ref[i, o * 8 : o * 8 + 8, lanes] for i in range(6)]
            terms = [rows[i] * rows[j] for i, j in index_pairs] + [rows[i] * rows[5] for i in range(5)]
            sums = terms if o == 0 else [s + t for s, t in zip(sums, terms)]
        halves.append([column_sum(s) for s in sums])
    pieces = []
    for k in range(20):
        row = jnp.concatenate([half[k] for half in halves], axis=1)
        pieces.append(high * row)
    stacked = jnp.concatenate(pieces, axis=0)
    accumulate(acc_ref, packed_dot(stacked, low, 3), step)

    @pl.when(step == STEPS - 1)
    def _():
        for k in range(20):
            keep_ref[k] = acc_ref[k * 16 : k * 16 + 8]
            send_ref[k] = acc_ref[k * 16 + 8 : k * 16 + 16]


def shifted(rows, distance):
    moved = pltpu.roll(rows, distance, 1)
    below = pltpu.roll(moved, 1, 0)
    row = lax.broadcasted_iota(jnp.int32, rows.shape, 0)
    lane = lax.broadcasted_iota(jnp.int32, rows.shape, 1)
    return jnp.where(lane >= distance, moved, jnp.where(row > 0, below, 0.0))


def knots_of(parts):
    total = parts[0]
    for j in range(1, 4):
        total = total + shifted(parts[j], j)
    return total


def diag_kernel(
    live_ref, att_ref, pha_ref, cal_ref, seg_ref, unit_ref,
    extra_ref, rank_ref, knots_ref, slots_ref, acc_ref, slot_ref, carry_ref,
):
    step = pl.program_id(0)
    live = live_row(live_ref, step)
    for c in range(4):
        for h in range(NB // 128):
            rows = att_ref[pl.ds(h * 512 + c, 128, stride=4), :]
            extra_ref[c, :, h * 128 : (h + 1) * 128] = rows.T
    extra_ref[4] = pha_ref[...].T
    extra_ref[5] = cal_ref[...].T
    seg = seg_ref[0]
    seg_high = rows_equal(8, seg >> 8) * live
    seg_low = narrow_rows_equal(256, seg & 255)
    halves = []
    for h in range(NB // 128):
        lanes = slice(h * 128, (h + 1) * 128)
        sums = [None] * 17
        for o in range(OBS // 8):
            rows = [extra_ref[i, o * 8 : o * 8 + 8, lanes] for i in range(6)]
            basis = [b * b for b in spline_basis(rows[4])]
            squares = [rows[c] * rows[c] for c in range(4)]
            terms = [b * s for b in basis for s in squares] + [rows[5] * rows[5]]
            sums = terms if o == 0 else [s + t for s, t in zip(sums, terms)]
        halves.append([column_sum(s) for s in sums])
    sums = [jnp.concatenate([half[k] for half in halves], axis=1) for k in range(17)]
    stacked = jnp.concatenate([seg_high * sums[k] for k in range(16)], axis=0)
    accumulate(acc_ref, packed_dot(stacked, seg_low, 2), step)

    unit = unit_ref[0]
    owner = rows_equal(RANGES, unit >> 12)
    owner_low = owner.astype(BF16)
    before = lax.broadcasted_iota(jnp.int32, (NB, NB), 0) < lax.broadcasted_iota(jnp.int32, (NB, NB), 1)
    before = jnp.where(before, 1.0, 0.0).astype(BF16)
    earlier = dot_nn(owner_low, before) + jnp.where(step > 0, carry_ref[...], 0.0)
    rank = column_sum(owner * earlier)
    accumulate(carry_ref, dot_nn(owner_low, jnp.ones((NB, NB), BF16)), step)
    rank = rank.astype(jnp.int32)
    rank_ref[0] = rank
    place = rows_equal(CAP, rank)
    inner = (unit & (SHARE - 1)).astype(F32)
    stacked = jnp.concatenate([place * (sums[16] * live), place * inner], axis=0)
    accumulate(slot_ref, packed_dot(stacked, owner_low, 2), step)

    @pl.when(step == STEPS - 1)
    def _():
        for c in range(4):
            knots_ref[c] = knots_of([acc_ref[(j * 4 + c) * 8 : (j * 4 + c) * 8 + 8] for j in range(4)])
        slots_ref[...] = slot_ref[...]


def solve_kernel(a_ref, b_ref, c_ref, d_ref, out_ref):
    packed = [(a_ref[k] + c_ref[k]) + (b_ref[k] + d_ref[k]) for k in range(20)]
    matrix = {}
    for position, (i, j) in enumerate(index_pairs):
        matrix[i, j] = packed[position] + (1.0 if i == j else 0.0)
    factor = {}
    inverse = {}
    for i in range(5):
        for j in range(i + 1):
            running = matrix[j, i]
            for k in range(j):
                running = running - factor[i, k] * factor[j, k]
            if i == j:
                inverse[i] = 1.0 / jnp.sqrt(running)
            else:
                factor[i, j] = running * inverse[j]
    forward = []
    for i in range(5):
        running = packed[15 + i]
        for k in range(i):
            running = running - factor[i, k] * forward[k]
        forward.append(running * inverse[i])
    result = [None] * 5
    for i in reversed(range(5)):
        running = forward[i]
        for k in range(i + 1, 5):
            running = running - factor[k, i] * result[k]
        result[i] = running * inverse[i]
        out_ref[i] = result[i]


def apply_kernel(
    live_ref, srct_ref, extra_ref, idx_ref, seg_ref, unit_ref, rank_ref, mine_ref, other_ref,
    diag_ref, slots_ref, out_ref, update_ref, table_ref, acc_ref, slot_ref,
):
    step = pl.program_id(0)
    fov = lax.axis_index("fov")

    @pl.when(step == 0)
    def _():
        out_ref[...] = jnp.zeros_like(out_ref)
        pieces = []
        for k in range(5):
            mine = mine_ref[k]
            other = other_ref[k]
            pieces += [mine, other]
            first = jnp.where(fov == 0, mine, other)
            second = jnp.where(fov == 0, other, mine)
            for q in range(8):
                update_ref[k : k + 1, q * 256 : (q + 1) * 256] = first[q : q + 1]
                update_ref[k : k + 1, 2048 + q * 256 : 2048 + (q + 1) * 256] = second[q : q + 1]
        stacked = jnp.concatenate(pieces, axis=0)
        table_ref[...] = jnp.concatenate(split_parts(stacked, 3), axis=1)

    live = live_row(live_ref, step)
    idx = idx_ref[0] ^ (fov * 2048)
    high = rows_equal(16, idx >> 8)
    low = narrow_rows_equal(256, idx & 255)
    looked = dot_nn(table_ref[...], jnp.concatenate([low] * 3, axis=0))
    chosen = [column_sum(looked[k * 16 : k * 16 + 16] * high) for k in range(5)]
    halves = []
    for h in range(NB // 128):
        lanes = slice(h * 128, (h + 1) * 128)
        spread = [jnp.broadcast_to(chosen[k][:, lanes], (8, 128)) for k in range(5)]
        sums = [None] * 17
        for o in range(OBS // 8):
            span = slice(o * 8, o * 8 + 8)
            model = srct_ref[0, span, lanes] * spread[0]
            for k in range(1, 5):
                model = model + srct_ref[k, span, lanes] * spread[k]
            residual = srct_ref[5, span, lanes] - model
            phase = extra_ref[4, span, lanes]
            moments = [extra_ref[c, span, lanes] * residual for c in range(4)]
            terms = list(moments)
            for _ in range(3):
                moments = [m * phase for m in moments]
                terms += moments
            terms.append(extra_ref[5, span, lanes] * residual)
            sums = terms if o == 0 else [s + t for s, t in zip(sums, terms)]
        halves.append([column_sum(s) for s in sums])
    sums = [jnp.concatenate([half[k] for half in halves], axis=1) for k in range(17)]
    seg = seg_ref[0]
    seg_high = rows_equal(8, seg >> 8) * live
    seg_low = narrow_rows_equal(256, seg & 255)
    stacked = jnp.concatenate([seg_high * sums[k] for k in range(16)], axis=0)
    accumulate(acc_ref, packed_dot(stacked, seg_low, 2), step)
    owner = narrow_rows_equal(RANGES, unit_ref[0] >> 12)
    placed = rows_equal(CAP, rank_ref[0]) * (sums[16] * live)
    accumulate(slot_ref, packed_dot(placed, owner, 2), step)

    @pl.when(step == STEPS - 1)
    def _():
        tm = lax.axis_index("tm")
        slots = jnp.concatenate([slot_ref[...], slots_ref[...], jnp.zeros((CAP, RANGES), F32)], axis=0)
        out_ref[pl.ds(0, RANGES, stride=PIECES), :] = slots.T
        first_half = lax.broadcasted_iota(jnp.int32, (8, 128), 1) < 64
        for c in range(4):
            moments = [acc_ref[(k * 4 + c) * 8 : (k * 4 + c) * 8 + 8] for k in range(4)]
            right = knots_of([spline_from_moments(moments, j) for j in range(4)])
            for r in range(2):
                columns = slice(r * 128, (r + 1) * 128)
                near, far = right[:, columns], diag_ref[c, :, columns]
                start = (r * 8 + tm * 2) * PIECES + 1 + c
                out_ref[pl.ds(start, 8, stride=16 * PIECES), :] = jnp.where(first_half, near, pltpu.roll(far, 64, 1))
                out_ref[pl.ds(start + PIECES, 8, stride=16 * PIECES), :] = jnp.where(
                    first_half, pltpu.roll(far, 64, 1), near
                )


def attitude_kernel(in_ref, att_ref):
    base = lax.axis_index("tm") * 2 * PIECES + 1
    knots = None
    for s in range(16):
        for f in range(2):
            part = in_ref[pl.ds(base + (s * 8 + f) * PIECES, 4), :]
            knots = part if knots is None else knots + part
    lower = lax.broadcasted_iota(jnp.int32, (4, 128), 1) < 64
    mine = lower == (lax.axis_index("fov") == 0)
    att_ref[...] = jnp.where(mine, knots / (1.0 + pltpu.roll(knots, 64, 1)), 0.0)


def calibration_kernel(in_ref, cal_ref, left_ref, right_ref):
    slots = in_ref[pl.ds(0, RANGES, stride=PIECES), :].T
    unit = slots[64:96].astype(jnp.int32)
    for k in range(CAP):
        lanes = slice(k * 128, (k + 1) * 128)
        inner = unit[k : k + 1]
        right_ref[:, lanes] = narrow_rows_equal(128, inner & 127)
        high = rows_equal(32, inner >> 7)
        stacked = jnp.concatenate([high * slots[k : k + 1], high * slots[32 + k : 33 + k]], axis=0)
        left_ref[:, lanes] = jnp.concatenate(split_parts(stacked, 2), axis=0)
    sums = dot_nt(left_ref[...], right_ref[...])
    sums = sums[:64] + sums[64:]
    cal_ref[...] = sums[:32] / (1.0 + sums[32:])


VMEM = pl.BlockSpec(memory_space=pltpu.VMEM)
SMEM = pl.BlockSpec(memory_space=pltpu.SMEM)
ROW = pl.BlockSpec((1, 1, NB), lambda s: (s, 0, 0))


def on_chip(*arrays):
    return [pltpu.with_memory_space_constraint(a, pltpu.VMEM) for a in arrays]


def whole(shape):
    return pl.BlockSpec(shape, lambda s: (0,) * len(shape))


def shards(
    src_partials,
    att_partials,
    cal_partials,
    obs_phase,
    obs_residual,
    block_source,
    block_segment,
    block_unit,
    live_blocks,
):
    source = block_source.reshape(STEPS, 1, NB)
    segment = block_segment.reshape(STEPS, 1, NB)
    unit = block_unit.reshape(STEPS, 1, NB)
    src = jnp.transpose(src_partials, (1, 0, 2))
    att = att_partials.reshape(BLK * 4, OBS)
    sequential = pltpu.CompilerParams(dimension_semantics=("arbitrary",))
    keep, send, srct = pl.pallas_call(
        normals_kernel,
        grid=(STEPS,),
        in_specs=[
            SMEM,
            pl.BlockSpec((5, NB, OBS), lambda s: (0, s, 0)),
            pl.BlockSpec((NB, OBS), lambda s: (s, 0)),
            ROW,
        ],
        out_specs=[
            VMEM,
            VMEM,
            pl.BlockSpec((6, OBS, NB), lambda s: (0, 0, s)),
        ],
        out_shape=[
            pltpu.VMEM((20, 8, 256), F32),
            pltpu.VMEM((20, 8, 256), F32),
            jax.ShapeDtypeStruct((6, OBS, BLK), F32),
        ],
        scratch_shapes=[pltpu.VMEM((320, 256), F32)],
        compiler_params=sequential,
        name="normals",
    )(live_blocks, src, obs_residual, source)
    half = keep + lax.ppermute(send, "fov", [(0, 1), (1, 0)])
    half, live_later = lax.optimization_barrier((half, live_blocks))
    around = [lax.ppermute(half, "tm", [(i, (i + d) % 4) for i in range(4)]) for d in (1, 2, 3)]
    extra, rank, diag_knots, diag_slots = pl.pallas_call(
        diag_kernel,
        grid=(STEPS,),
        in_specs=[
            SMEM,
            pl.BlockSpec((NB * 4, OBS), lambda s: (s, 0)),
            pl.BlockSpec((NB, OBS), lambda s: (s, 0)),
            pl.BlockSpec((NB, OBS), lambda s: (s, 0)),
            ROW,
            ROW,
        ],
        out_specs=[
            pl.BlockSpec((6, OBS, NB), lambda s: (0, 0, s)),
            ROW,
            VMEM,
            VMEM,
        ],
        out_shape=[
            jax.ShapeDtypeStruct((6, OBS, BLK), F32),
            jax.ShapeDtypeStruct((STEPS, 1, NB), jnp.int32),
            pltpu.VMEM((4, 8, 256), F32),
            pltpu.VMEM((64, RANGES), F32),
        ],
        scratch_shapes=[
            pltpu.VMEM((128, 256), F32),
            pltpu.VMEM((64, RANGES), F32),
            pltpu.VMEM((RANGES, NB), F32),
        ],
        compiler_params=sequential,
        cost_estimate=pl.CostEstimate(flops=200_000_000, bytes_accessed=12_000_000, transcendentals=0),
        name="diag",
    )(live_later, att, obs_phase, cal_partials, segment, unit)
    around, diag_knots = lax.optimization_barrier((around, diag_knots))
    mine = pl.pallas_call(
        solve_kernel,
        in_specs=[VMEM] * 4,
        out_specs=VMEM,
        out_shape=pltpu.VMEM((5, 8, 256), F32),
        name="solve",
    )(*on_chip(half, *around))
    other = lax.ppermute(mine, "fov", [(0, 1), (1, 0)])
    outgoing, src_update = pl.pallas_call(
        apply_kernel,
        grid=(STEPS,),
        in_specs=[
            SMEM,
            pl.BlockSpec((6, OBS, NB), lambda s: (0, 0, s)),
            pl.BlockSpec((6, OBS, NB), lambda s: (0, 0, s)),
            ROW,
            ROW,
            ROW,
            ROW,
            VMEM,
            VMEM,
            VMEM,
            VMEM,
        ],
        out_specs=[VMEM, whole((5, 4096))],
        out_shape=[
            pltpu.VMEM((128 * PIECES, 128), F32),
            jax.ShapeDtypeStruct((5, 4096), F32),
        ],
        scratch_shapes=[
            pltpu.VMEM((80, 768), BF16),
            pltpu.VMEM((128, 256), F32),
            pltpu.VMEM((CAP, RANGES), F32),
        ],
        compiler_params=sequential,
        name="apply",
    )(live_blocks, srct, extra, source, segment, unit, rank, *on_chip(mine, other, diag_knots, diag_slots))
    arrived = lax.all_to_all(
        outgoing.reshape(128, 1, PIECES * 128), ALL, split_axis=0, concat_axis=0, tiled=True
    ).reshape(128 * PIECES, 128)
    att_half = pl.pallas_call(
        attitude_kernel,
        in_specs=[VMEM],
        out_specs=VMEM,
        out_shape=pltpu.VMEM((4, 128), F32),
        name="attitude",
    )(*on_chip(arrived))
    att_other = lax.ppermute(att_half, "fov", [(0, 1), (1, 0)])
    cal_update = pl.pallas_call(
        calibration_kernel,
        in_specs=[VMEM],
        out_specs=VMEM,
        out_shape=jax.ShapeDtypeStruct((32, 128), F32),
        scratch_shapes=[pltpu.VMEM((128, CAP * 128), BF16), pltpu.VMEM((128, CAP * 128), BF16)],
        cost_estimate=pl.CostEstimate(flops=100_000_000, bytes_accessed=400_000, transcendentals=0),
        name="calibration",
    )(*on_chip(arrived))
    att_update = att_half + att_other
    return (src_update, att_update.reshape(4, 1, 128), cal_update.reshape(SHARE))


def solution(mesh):
    return jax.shard_map(
        shards,
        mesh=mesh,
        in_specs=(
            P(ALL, None, None),
            P(ALL, None, None),
            P(ALL, None),
            P(ALL, None),
            P(ALL, None),
            P(ALL),
            P(ALL),
            P(ALL),
            P(ALL),
        ),
        out_specs=(P(None, "sky"), P(None, "tm", "sky"), P(ALL)),
        check_vma=False,
    )
```

```python
import jax
import jax.numpy as jnp
from jax import lax
from jax.experimental import pallas as pl
from jax.experimental.pallas import tpu as pltpu
from jax.sharding import PartitionSpec as P

BLK = 2048
NB = 256
STEPS = BLK // NB
OBS = 128
CAP = 32
RANGES = 128
SHARE = 4096
PIECES = 5
F32 = jnp.float32
BF16 = jnp.bfloat16
ALL = ("sky", "tm", "fov")

index_pairs = [(i, j) for i in range(5) for j in range(i, 5)]


def split_parts(x, count):
    parts = []
    for _ in range(count - 1):
        part = x.astype(BF16)
        parts.append(part)
        x = x - part.astype(F32)
    parts.append(x.astype(BF16))
    return parts


def dot_nt(a, b):
    return lax.dot_general(a, b, (((1,), (1,)), ((), ())), preferred_element_type=F32)


def dot_nn(a, b):
    return lax.dot_general(a, b, (((1,), (0,)), ((), ())), preferred_element_type=F32)


def packed_dot(left, right, count):
    return dot_nt(
        jnp.concatenate(split_parts(left, count), axis=1), jnp.concatenate([right] * count, axis=1)
    )


def rows_equal(count, row):
    iota = lax.broadcasted_iota(jnp.int32, (count, row.shape[1]), 0)
    return jnp.where(iota == row, 1.0, 0.0)


def narrow_rows_equal(count, row):
    iota = lax.broadcasted_iota(jnp.int32, (count, row.shape[1]), 0).astype(F32).astype(BF16)
    wide = jnp.broadcast_to(row.astype(F32), (count, row.shape[1])).astype(BF16)
    return jnp.where(iota == wide, jnp.ones((), BF16), jnp.zeros((), BF16))


def accumulate(ref, product, step):
    @pl.when(step == 0)
    def _():
        ref[...] = product

    @pl.when(step > 0)
    def _():
        ref[...] += product


def live_row(live_ref, step):
    position = step * NB + lax.broadcasted_iota(jnp.int32, (1, NB), 1)
    return jnp.where(position < live_ref[0], 1.0, 0.0)


def columns_of(ref, step):
    return ref.at[:, :, pl.ds(pl.multiple_of(step * NB, NB), NB)]


def column_sum(x):
    return jnp.sum(x, axis=0, keepdims=True)


def spline_basis(phase):
    rest = 1.0 - phase
    square = phase * phase
    cubed = square * phase
    half = 0.5 * cubed
    return (
        rest * rest * rest * (1.0 / 6.0),
        half - square + (2.0 / 3.0),
        0.5 * (square + phase) - half + (1.0 / 6.0),
        cubed * (1.0 / 6.0),
    )


def spline_from_moments(m, j):
    sixth = 1.0 / 6.0
    if j == 0:
        return (m[0] - m[3]) * sixth + 0.5 * (m[2] - m[1])
    if j == 1:
        return m[0] * (2.0 / 3.0) - m[2] + 0.5 * m[3]
    if j == 2:
        return m[0] * sixth + 0.5 * (m[1] + m[2] - m[3])
    return m[3] * sixth


def normals_kernel(live_ref, src_ref, res_ref, idx_ref, keep_ref, send_ref, all_src_ref, acc_ref):
    step = pl.program_id(0)
    srct_ref = columns_of(all_src_ref, step)
    for i in range(5):
        srct_ref[i] = src_ref[i].T
    srct_ref[5] = res_ref[...].T
    idx = idx_ref[0] ^ (lax.axis_index("fov") * 2048)
    high = rows_equal(16, idx >> 8) * live_row(live_ref, step)
    low = narrow_rows_equal(256, idx & 255)
    halves = []
    for h in range(NB // 128):
        lanes = slice(h * 128, (h + 1) * 128)
        sums = [None] * 20
        for o in range(OBS // 8):
            rows = [srct_ref[i, o * 8 : o * 8 + 8, lanes] for i in range(6)]
            terms = [rows[i] * rows[j] for i, j in index_pairs] + [rows[i] * rows[5] for i in range(5)]
            sums = terms if o == 0 else [s + t for s, t in zip(sums, terms)]
        halves.append([column_sum(s) for s in sums])
    pieces = []
    for k in range(20):
        row = jnp.concatenate([half[k] for half in halves], axis=1)
        pieces.append(high * row)
    stacked = jnp.concatenate(pieces, axis=0)
    accumulate(acc_ref, packed_dot(stacked, low, 3), step)

    @pl.when(step == STEPS - 1)
    def _():
        for k in range(20):
            keep_ref[k] = acc_ref[k * 16 : k * 16 + 8]
            send_ref[k] = acc_ref[k * 16 + 8 : k * 16 + 16]


def shifted(rows, distance):
    moved = pltpu.roll(rows, distance, 1)
    below = pltpu.roll(moved, 1, 0)
    row = lax.broadcasted_iota(jnp.int32, rows.shape, 0)
    lane = lax.broadcasted_iota(jnp.int32, rows.shape, 1)
    return jnp.where(lane >= distance, moved, jnp.where(row > 0, below, 0.0))


def knots_of(parts):
    total = parts[0]
    for j in range(1, 4):
        total = total + shifted(parts[j], j)
    return total


def diag_kernel(
    live_ref, att_ref, pha_ref, cal_ref, seg_ref, unit_ref,
    all_extra_ref, rank_ref, knots_ref, slots_ref, acc_ref, slot_ref, carry_ref,
):
    step = pl.program_id(0)
    extra_ref = columns_of(all_extra_ref, step)
    live = live_row(live_ref, step)
    for c in range(4):
        for h in range(NB // 128):
            rows = att_ref[pl.ds(h * 512 + c, 128, stride=4), :]
            extra_ref[c, :, h * 128 : (h + 1) * 128] = rows.T
    extra_ref[4] = pha_ref[...].T
    extra_ref[5] = cal_ref[...].T
    seg = seg_ref[0]
    seg_high = rows_equal(8, seg >> 8) * live
    seg_low = narrow_rows_equal(256, seg & 255)
    halves = []
    for h in range(NB // 128):
        lanes = slice(h * 128, (h + 1) * 128)
        sums = [None] * 17
        for o in range(OBS // 8):
            rows = [extra_ref[i, o * 8 : o * 8 + 8, lanes] for i in range(6)]
            basis = [b * b for b in spline_basis(rows[4])]
            squares = [rows[c] * rows[c] for c in range(4)]
            terms = [b * s for b in basis for s in squares] + [rows[5] * rows[5]]
            sums = terms if o == 0 else [s + t for s, t in zip(sums, terms)]
        halves.append([column_sum(s) for s in sums])
    sums = [jnp.concatenate([half[k] for half in halves], axis=1) for k in range(17)]
    stacked = jnp.concatenate([seg_high * sums[k] for k in range(16)], axis=0)
    accumulate(acc_ref, packed_dot(stacked, seg_low, 2), step)

    unit = unit_ref[0]
    owner = rows_equal(RANGES, unit >> 12)
    owner_low = owner.astype(BF16)
    before = lax.broadcasted_iota(jnp.int32, (NB, NB), 0) < lax.broadcasted_iota(jnp.int32, (NB, NB), 1)
    before = jnp.where(before, 1.0, 0.0).astype(BF16)
    earlier = dot_nn(owner_low, before) + jnp.where(step > 0, carry_ref[...], 0.0)
    rank = column_sum(owner * earlier)
    accumulate(carry_ref, dot_nn(owner_low, jnp.ones((NB, NB), BF16)), step)
    rank = rank.astype(jnp.int32)
    rank_ref[0] = rank
    place = rows_equal(CAP, rank)
    inner = (unit & (SHARE - 1)).astype(F32)
    stacked = jnp.concatenate([place * (sums[16] * live), place * inner], axis=0)
    accumulate(slot_ref, packed_dot(stacked, owner_low, 2), step)

    @pl.when(step == STEPS - 1)
    def _():
        for c in range(4):
            knots_ref[c] = knots_of([acc_ref[(j * 4 + c) * 8 : (j * 4 + c) * 8 + 8] for j in range(4)])
        slots_ref[...] = slot_ref[...]


def join_kernel(a_ref, b_ref, out_ref):
    out_ref[...] = a_ref[...] + b_ref[...]


def solve_kernel(a_ref, b_ref, c_ref, d_ref, out_ref):
    packed = [(a_ref[k] + c_ref[k]) + (b_ref[k] + d_ref[k]) for k in range(20)]
    matrix = {}
    for position, (i, j) in enumerate(index_pairs):
        matrix[i, j] = packed[position] + (1.0 if i == j else 0.0)
    factor = {}
    inverse = {}
    for i in range(5):
        for j in range(i + 1):
            running = matrix[j, i]
            for k in range(j):
                running = running - factor[i, k] * factor[j, k]
            if i == j:
                inverse[i] = 1.0 / jnp.sqrt(running)
            else:
                factor[i, j] = running * inverse[j]
    forward = []
    for i in range(5):
        running = packed[15 + i]
        for k in range(i):
            running = running - factor[i, k] * forward[k]
        forward.append(running * inverse[i])
    result = [None] * 5
    for i in reversed(range(5)):
        running = forward[i]
        for k in range(i + 1, 5):
            running = running - factor[k, i] * result[k]
        result[i] = running * inverse[i]
        out_ref[i] = result[i]


def apply_kernel(
    live_ref, all_src_ref, all_extra_ref, idx_ref, seg_ref, unit_ref, rank_ref, mine_ref, other_ref,
    diag_ref, slots_ref, out_ref, update_ref, table_ref, acc_ref, slot_ref,
):
    step = pl.program_id(0)
    srct_ref = columns_of(all_src_ref, step)
    extra_ref = columns_of(all_extra_ref, step)
    fov = lax.axis_index("fov")

    @pl.when(step == 0)
    def _():
        out_ref[...] = jnp.zeros_like(out_ref)
        pieces = []
        for k in range(5):
            mine = mine_ref[k]
            other = other_ref[k]
            pieces += [mine, other]
            first = jnp.where(fov == 0, mine, other)
            second = jnp.where(fov == 0, other, mine)
            for q in range(8):
                update_ref[k : k + 1, q * 256 : (q + 1) * 256] = first[q : q + 1]
                update_ref[k : k + 1, 2048 + q * 256 : 2048 + (q + 1) * 256] = second[q : q + 1]
        stacked = jnp.concatenate(pieces, axis=0)
        table_ref[...] = jnp.concatenate(split_parts(stacked, 3), axis=1)

    live = live_row(live_ref, step)
    idx = idx_ref[0] ^ (fov * 2048)
    high = rows_equal(16, idx >> 8)
    low = narrow_rows_equal(256, idx & 255)
    looked = dot_nn(table_ref[...], jnp.concatenate([low] * 3, axis=0))
    chosen = [column_sum(looked[k * 16 : k * 16 + 16] * high) for k in range(5)]
    halves = []
    for h in range(NB // 128):
        lanes = slice(h * 128, (h + 1) * 128)
        spread = [jnp.broadcast_to(chosen[k][:, lanes], (8, 128)) for k in range(5)]
        sums = [None] * 17
        for o in range(OBS // 8):
            span = slice(o * 8, o * 8 + 8)
            model = srct_ref[0, span, lanes] * spread[0]
            for k in range(1, 5):
                model = model + srct_ref[k, span, lanes] * spread[k]
            residual = srct_ref[5, span, lanes] - model
            phase = extra_ref[4, span, lanes]
            moments = [extra_ref[c, span, lanes] * residual for c in range(4)]
            terms = list(moments)
            for _ in range(3):
                moments = [m * phase for m in moments]
                terms += moments
            terms.append(extra_ref[5, span, lanes] * residual)
            sums = terms if o == 0 else [s + t for s, t in zip(sums, terms)]
        halves.append([column_sum(s) for s in sums])
    sums = [jnp.concatenate([half[k] for half in halves], axis=1) for k in range(17)]
    seg = seg_ref[0]
    seg_high = rows_equal(8, seg >> 8) * live
    seg_low = narrow_rows_equal(256, seg & 255)
    stacked = jnp.concatenate([seg_high * sums[k] for k in range(16)], axis=0)
    accumulate(acc_ref, packed_dot(stacked, seg_low, 2), step)
    owner = narrow_rows_equal(RANGES, unit_ref[0] >> 12)
    placed = rows_equal(CAP, rank_ref[0]) * (sums[16] * live)
    accumulate(slot_ref, packed_dot(placed, owner, 2), step)

    @pl.when(step == STEPS - 1)
    def _():
        tm = lax.axis_index("tm")
        slots = jnp.concatenate([slot_ref[...], slots_ref[...], jnp.zeros((CAP, RANGES), F32)], axis=0)
        out_ref[pl.ds(0, RANGES, stride=PIECES), :] = slots.T
        first_half = lax.broadcasted_iota(jnp.int32, (8, 128), 1) < 64
        for c in range(4):
            moments = [acc_ref[(k * 4 + c) * 8 : (k * 4 + c) * 8 + 8] for k in range(4)]
            right = knots_of([spline_from_moments(moments, j) for j in range(4)])
            for r in range(2):
                columns = slice(r * 128, (r + 1) * 128)
                near, far = right[:, columns], diag_ref[c, :, columns]
                start = (r * 8 + tm * 2) * PIECES + 1 + c
                out_ref[pl.ds(start, 8, stride=16 * PIECES), :] = jnp.where(first_half, near, pltpu.roll(far, 64, 1))
                out_ref[pl.ds(start + PIECES, 8, stride=16 * PIECES), :] = jnp.where(
                    first_half, pltpu.roll(far, 64, 1), near
                )


def attitude_kernel(in_ref, att_ref):
    base = lax.axis_index("tm") * 2 * PIECES + 1
    knots = None
    for s in range(16):
        for f in range(2):
            part = in_ref[pl.ds(base + (s * 8 + f) * PIECES, 4), :]
            knots = part if knots is None else knots + part
    lower = lax.broadcasted_iota(jnp.int32, (4, 128), 1) < 64
    mine = lower == (lax.axis_index("fov") == 0)
    att_ref[...] = jnp.where(mine, knots / (1.0 + pltpu.roll(knots, 64, 1)), 0.0)


def calibration_kernel(in_ref, cal_ref, left_ref, right_ref):
    slots = in_ref[pl.ds(0, RANGES, stride=PIECES), :].T
    unit = slots[64:96].astype(jnp.int32)
    for k in range(CAP):
        lanes = slice(k * 128, (k + 1) * 128)
        inner = unit[k : k + 1]
        right_ref[:, lanes] = narrow_rows_equal(128, inner & 127)
        high = rows_equal(32, inner >> 7)
        stacked = jnp.concatenate([high * slots[k : k + 1], high * slots[32 + k : 33 + k]], axis=0)
        left_ref[:, lanes] = jnp.concatenate(split_parts(stacked, 2), axis=0)
    sums = dot_nt(left_ref[...], right_ref[...])
    sums = sums[:64] + sums[64:]
    cal_ref[...] = sums[:32] / (1.0 + sums[32:])


VMEM = pl.BlockSpec(memory_space=pltpu.VMEM)
SMEM = pl.BlockSpec(memory_space=pltpu.SMEM)
ROW = pl.BlockSpec((1, 1, NB), lambda s: (s, 0, 0))


def on_chip(*arrays):
    return [pltpu.with_memory_space_constraint(a, pltpu.VMEM) for a in arrays]


def off_chip(*arrays):
    return [pltpu.with_memory_space_constraint(a, pltpu.HBM) for a in arrays]


def whole(shape):
    return pl.BlockSpec(shape, lambda s: (0,) * len(shape))


def shards(
    src_partials,
    att_partials,
    cal_partials,
    obs_phase,
    obs_residual,
    block_source,
    block_segment,
    block_unit,
    live_blocks,
):
    source = block_source.reshape(STEPS, 1, NB)
    segment = block_segment.reshape(STEPS, 1, NB)
    unit = block_unit.reshape(STEPS, 1, NB)
    src = jnp.transpose(src_partials, (1, 0, 2))
    att = att_partials.reshape(BLK * 4, OBS)
    sequential = pltpu.CompilerParams(dimension_semantics=("arbitrary",), vmem_limit_bytes=24 * 1024 * 1024)
    small = pltpu.CompilerParams(vmem_limit_bytes=4 * 1024 * 1024)
    keep, send, srct = pl.pallas_call(
        normals_kernel,
        grid=(STEPS,),
        in_specs=[
            SMEM,
            pl.BlockSpec((5, NB, OBS), lambda s: (0, s, 0)),
            pl.BlockSpec((NB, OBS), lambda s: (s, 0)),
            ROW,
        ],
        out_specs=[
            VMEM,
            VMEM,
            VMEM,
        ],
        out_shape=[
            pltpu.VMEM((20, 8, 256), F32),
            pltpu.VMEM((20, 8, 256), F32),
            pltpu.VMEM((6, OBS, BLK), F32),
        ],
        scratch_shapes=[pltpu.VMEM((320, 256), F32)],
        compiler_params=sequential,
        name="normals",
    )(live_blocks, *off_chip(src, obs_residual, source))
    half = pl.pallas_call(
        join_kernel,
        in_specs=[VMEM] * 2,
        out_specs=VMEM,
        out_shape=pltpu.VMEM((20, 8, 256), F32),
        compiler_params=small,
        name="join",
    )(*on_chip(keep, lax.ppermute(send, "fov", [(0, 1), (1, 0)])))
    half, live_later = lax.optimization_barrier((half, live_blocks))
    around = [lax.ppermute(half, "tm", [(i, (i + d) % 4) for i in range(4)]) for d in (1, 2, 3)]
    extra, rank, diag_knots, diag_slots = pl.pallas_call(
        diag_kernel,
        grid=(STEPS,),
        in_specs=[
            SMEM,
            pl.BlockSpec((NB * 4, OBS), lambda s: (s, 0)),
            pl.BlockSpec((NB, OBS), lambda s: (s, 0)),
            pl.BlockSpec((NB, OBS), lambda s: (s, 0)),
            ROW,
            ROW,
        ],
        out_specs=[
            VMEM,
            ROW,
            VMEM,
            VMEM,
        ],
        out_shape=[
            pltpu.VMEM((6, OBS, BLK), F32),
            jax.ShapeDtypeStruct((STEPS, 1, NB), jnp.int32),
            pltpu.VMEM((4, 8, 256), F32),
            pltpu.VMEM((64, RANGES), F32),
        ],
        scratch_shapes=[
            pltpu.VMEM((128, 256), F32),
            pltpu.VMEM((64, RANGES), F32),
            pltpu.VMEM((RANGES, NB), F32),
        ],
        compiler_params=sequential,
        cost_estimate=pl.CostEstimate(flops=200_000_000, bytes_accessed=12_000_000, transcendentals=0),
        name="diag",
    )(live_later, att, obs_phase, cal_partials, segment, unit)
    around, diag_knots = lax.optimization_barrier((around, diag_knots))
    mine = pl.pallas_call(
        solve_kernel,
        in_specs=[VMEM] * 4,
        out_specs=VMEM,
        out_shape=pltpu.VMEM((5, 8, 256), F32),
        compiler_params=small,
        name="solve",
    )(*on_chip(half, *around))
    other = lax.ppermute(mine, "fov", [(0, 1), (1, 0)])
    outgoing, src_update = pl.pallas_call(
        apply_kernel,
        grid=(STEPS,),
        in_specs=[
            SMEM,
            VMEM,
            VMEM,
            ROW,
            ROW,
            ROW,
            ROW,
            VMEM,
            VMEM,
            VMEM,
            VMEM,
        ],
        out_specs=[VMEM, whole((5, 4096))],
        out_shape=[
            pltpu.VMEM((128 * PIECES, 128), F32),
            jax.ShapeDtypeStruct((5, 4096), F32),
        ],
        scratch_shapes=[
            pltpu.VMEM((80, 768), BF16),
            pltpu.VMEM((128, 256), F32),
            pltpu.VMEM((CAP, RANGES), F32),
        ],
        compiler_params=sequential,
        name="apply",
    )(live_blocks, *on_chip(srct, extra), source, segment, unit, rank, *on_chip(mine, other, diag_knots, diag_slots))
    arrived = lax.all_to_all(
        outgoing.reshape(128, 1, PIECES * 128), ALL, split_axis=0, concat_axis=0, tiled=True
    ).reshape(128 * PIECES, 128)
    att_half = pl.pallas_call(
        attitude_kernel,
        in_specs=[VMEM],
        out_specs=VMEM,
        out_shape=pltpu.VMEM((4, 128), F32),
        compiler_params=small,
        name="attitude",
    )(*on_chip(arrived))
    att_other = lax.ppermute(att_half, "fov", [(0, 1), (1, 0)])
    cal_update = pl.pallas_call(
        calibration_kernel,
        in_specs=[VMEM],
        out_specs=VMEM,
        out_shape=jax.ShapeDtypeStruct((32, 128), F32),
        scratch_shapes=[pltpu.VMEM((128, CAP * 128), BF16), pltpu.VMEM((128, CAP * 128), BF16)],
        cost_estimate=pl.CostEstimate(flops=100_000_000, bytes_accessed=400_000, transcendentals=0),
        name="calibration",
    )(*on_chip(arrived))
    att_update = att_half + att_other
    return (src_update, att_update.reshape(4, 1, 128), cal_update.reshape(SHARE))


def solution(mesh):
    return jax.shard_map(
        shards,
        mesh=mesh,
        in_specs=(
            P(ALL, None, None),
            P(ALL, None, None),
            P(ALL, None),
            P(ALL, None),
            P(ALL, None),
            P(ALL),
            P(ALL),
            P(ALL),
            P(ALL),
        ),
        out_specs=(P(None, "sky"), P(None, "tm", "sky"), P(ALL)),
        check_vma=False,
    )
```

```python
import jax
import jax.numpy as jnp
from jax import lax
from jax.experimental import pallas as pl
from jax.experimental.pallas import tpu as pltpu
from jax.sharding import PartitionSpec as P

BLK = 2048
NB = 256
STEPS = BLK // NB
WIDE = 512
WIDE_STEPS = BLK // WIDE
OBS = 128
CAP = 32
RANGES = 128
SHARE = 4096
PIECES = 5
F32 = jnp.float32
BF16 = jnp.bfloat16
ALL = ("sky", "tm", "fov")

index_pairs = [(i, j) for i in range(5) for j in range(i, 5)]


def split_parts(x, count):
    parts = []
    for _ in range(count - 1):
        part = x.astype(BF16)
        parts.append(part)
        x = x - part.astype(F32)
    parts.append(x.astype(BF16))
    return parts


def dot_nt(a, b):
    return lax.dot_general(a, b, (((1,), (1,)), ((), ())), preferred_element_type=F32)


def dot_nn(a, b):
    return lax.dot_general(a, b, (((1,), (0,)), ((), ())), preferred_element_type=F32)


def rows_equal(count, row):
    iota = lax.broadcasted_iota(jnp.int32, (count, row.shape[1]), 0)
    return jnp.where(iota == row, 1.0, 0.0)


def narrow_rows_equal(count, row):
    iota = lax.broadcasted_iota(jnp.int32, (count, row.shape[1]), 0).astype(F32).astype(BF16)
    wide = jnp.broadcast_to(row.astype(F32), (count, row.shape[1])).astype(BF16)
    return jnp.where(iota == wide, jnp.ones((), BF16), jnp.zeros((), BF16))


def accumulate(ref, product, step):
    @pl.when(step == 0)
    def _():
        ref[...] = product

    @pl.when(step > 0)
    def _():
        ref[...] += product


def live_row(live_ref, step, width):
    position = step * width + lax.broadcasted_iota(jnp.int32, (1, width), 1)
    return jnp.where(position < live_ref[0], 1.0, 0.0)


def columns(step, width):
    return pl.ds(pl.multiple_of(step * width, width), width)


def row_bit(bit):
    return (lax.broadcasted_iota(jnp.int32, (8, 128), 0) & bit) == 0


def fold(accs):
    upper = row_bit(4)
    level = [
        jnp.where(upper, accs[i], accs[i + 4]) + pltpu.roll(jnp.where(upper, accs[i + 4], accs[i]), 4, 0)
        for i in range(4)
    ]
    upper = row_bit(2)
    level = [
        jnp.where(upper, level[i], level[i + 2])
        + jnp.where(upper, pltpu.roll(level[i], 6, 0), pltpu.roll(level[i + 2], 2, 0))
        for i in range(2)
    ]
    upper = row_bit(1)
    return jnp.where(upper, level[0], level[1]) + jnp.where(
        upper, pltpu.roll(level[0], 7, 0), pltpu.roll(level[1], 1, 0)
    )


def wide_parts(x, count):
    parts = []
    for _ in range(count - 1):
        part = x.astype(BF16).astype(F32)
        parts.append(part)
        x = x - part
    return parts + [x]


def masked_rows(mask, blocks, count):
    sides = []
    split = [wide_parts(block, count) for block in blocks]
    for n in range(count):
        pieces = []
        for parts in split:
            for k in range(parts[n].shape[0]):
                pieces.append(mask * jnp.broadcast_to(parts[n][k : k + 1], mask.shape).astype(BF16))
        sides.append(jnp.concatenate(pieces, axis=0))
    return jnp.concatenate(sides, axis=1)


def repeated_dot(left, right, count):
    return dot_nt(left, jnp.concatenate([right] * count, axis=1))


def column_sum(x):
    return jnp.sum(x, axis=0, keepdims=True)


def spline_basis(phase):
    rest = 1.0 - phase
    square = phase * phase
    cubed = square * phase
    half = 0.5 * cubed
    return (
        rest * rest * rest * (1.0 / 6.0),
        half - square + (2.0 / 3.0),
        0.5 * (square + phase) - half + (1.0 / 6.0),
        cubed * (1.0 / 6.0),
    )


def spline_from_moments(m, j):
    sixth = 1.0 / 6.0
    if j == 0:
        return (m[0] - m[3]) * sixth + 0.5 * (m[2] - m[1])
    if j == 1:
        return m[0] * (2.0 / 3.0) - m[2] + 0.5 * m[3]
    if j == 2:
        return m[0] * sixth + 0.5 * (m[1] + m[2] - m[3])
    return m[3] * sixth


def normals_kernel(live_ref, src_ref, res_ref, idx_ref, keep_ref, send_ref, all_src_ref, all_low_ref, acc_ref):
    step = pl.program_id(0)
    span = columns(step, WIDE)
    srct_ref = all_src_ref.at[:, :, span]
    idx = idx_ref[0] ^ (lax.axis_index("fov") * 2048)
    high = (rows_equal(16, idx >> 8) * live_row(live_ref, step, WIDE)).astype(BF16)
    low = narrow_rows_equal(256, idx & 255)
    all_low_ref[:, span] = low
    groups = []
    spare = []
    for h in range(WIDE // 128):
        lanes = slice(h * 128, (h + 1) * 128)
        for i in range(5):
            srct_ref[i, :, lanes] = src_ref[i, lanes, :].T
        srct_ref[5, :, lanes] = res_ref[lanes, :].T
        sums = [None] * 20
        for o in range(OBS // 8):
            rows = [srct_ref[i, o * 8 : o * 8 + 8, lanes] for i in range(6)]
            terms = [rows[i] * rows[j] for i, j in index_pairs] + [rows[i] * rows[5] for i in range(5)]
            sums = terms if o == 0 else [s + t for s, t in zip(sums, terms)]
        groups.append(jnp.concatenate([fold(sums[:8]), fold(sums[8:16])], axis=0))
        spare.append(sums[16:])
    rest = []
    for h in range(0, WIDE // 128, 2):
        both = fold(spare[h] + spare[h + 1])
        rest += [both[:4], both[4:]]
    blocks = [jnp.concatenate(groups, axis=1), jnp.concatenate(rest, axis=1)]
    accumulate(acc_ref, repeated_dot(masked_rows(high, blocks, 3), low, 3), step)

    @pl.when(step == WIDE_STEPS - 1)
    def _():
        for k in range(20):
            keep_ref[k] = acc_ref[k * 16 : k * 16 + 8]
            send_ref[k] = acc_ref[k * 16 + 8 : k * 16 + 16]


def shifted(rows, distance):
    moved = pltpu.roll(rows, distance, 1)
    below = pltpu.roll(moved, 1, 0)
    row = lax.broadcasted_iota(jnp.int32, rows.shape, 0)
    lane = lax.broadcasted_iota(jnp.int32, rows.shape, 1)
    return jnp.where(lane >= distance, moved, jnp.where(row > 0, below, 0.0))


def knots_of(parts):
    total = parts[0]
    for j in range(1, 4):
        total = total + shifted(parts[j], j)
    return total


def diag_kernel(
    live_ref, att_ref, pha_ref, cal_ref, seg_ref, unit_ref,
    all_extra_ref, all_low_ref, all_owner_ref, all_high_ref, all_place_ref, knots_ref, slots_ref,
    acc_ref, slot_ref, carry_ref,
):
    step = pl.program_id(0)
    span = columns(step, NB)
    extra_ref = all_extra_ref.at[:, :, span]
    live = live_row(live_ref, step, NB)
    unit = unit_ref[0]
    owner = rows_equal(RANGES, unit >> 12)
    owner_low = owner.astype(BF16)
    all_owner_ref[:, span] = owner_low
    before = lax.broadcasted_iota(jnp.int32, (NB, NB), 0) < lax.broadcasted_iota(jnp.int32, (NB, NB), 1)
    before = jnp.where(before, 1.0, 0.0).astype(BF16)
    earlier = dot_nn(owner_low, before) + jnp.where(step > 0, carry_ref[...], 0.0)
    rank = column_sum(owner * earlier).astype(jnp.int32)
    accumulate(carry_ref, dot_nn(owner_low, jnp.ones((NB, NB), BF16)), step)
    place = rows_equal(CAP, rank)
    place_live = (place * live).astype(BF16)
    all_place_ref[:, span] = place_live
    seg = seg_ref[0]
    seg_high = (rows_equal(16, seg >> 7) * live).astype(BF16)
    seg_low = narrow_rows_equal(128, seg & 127)
    all_high_ref[:, span] = seg_high
    all_low_ref[:, span] = seg_low
    groups = []
    units = []
    for h in range(NB // 128):
        lanes = slice(h * 128, (h + 1) * 128)
        for c in range(4):
            extra_ref[c, :, lanes] = att_ref[pl.ds(h * 512 + c, 128, stride=4), :].T
        extra_ref[4, :, lanes] = pha_ref[lanes, :].T
        extra_ref[5, :, lanes] = cal_ref[lanes, :].T
        sums = [None] * 17
        for o in range(OBS // 8):
            rows = [extra_ref[i, o * 8 : o * 8 + 8, lanes] for i in range(6)]
            basis = [b * b for b in spline_basis(rows[4])]
            squares = [rows[c] * rows[c] for c in range(4)]
            terms = [b * s for b in basis for s in squares] + [rows[5] * rows[5]]
            sums = terms if o == 0 else [s + t for s, t in zip(sums, terms)]
        groups.append(jnp.concatenate([fold(sums[:8]), fold(sums[8:16])], axis=0))
        units.append(column_sum(sums[16]))
    left = masked_rows(seg_high, [jnp.concatenate(groups, axis=1)], 2)
    accumulate(acc_ref, repeated_dot(left, seg_low, 2), step)
    inner = (unit & (SHARE - 1)).astype(F32)
    left = jnp.concatenate(
        [
            masked_rows(place_live, [jnp.concatenate(units, axis=1)], 2),
            masked_rows(place.astype(BF16), [inner], 2),
        ],
        axis=0,
    )
    accumulate(slot_ref, repeated_dot(left, owner_low, 2), step)

    @pl.when(step == STEPS - 1)
    def _():
        for c in range(4):
            knots_ref[c] = knots_of([acc_ref[(j * 4 + c) * 16 : (j * 4 + c) * 16 + 16] for j in range(4)])
        slots_ref[...] = slot_ref[...]


def join_kernel(a_ref, b_ref, out_ref):
    out_ref[...] = a_ref[...] + b_ref[...]


def solve_kernel(a_ref, b_ref, c_ref, d_ref, out_ref):
    packed = [(a_ref[k] + c_ref[k]) + (b_ref[k] + d_ref[k]) for k in range(20)]
    matrix = {}
    for position, (i, j) in enumerate(index_pairs):
        matrix[i, j] = packed[position] + (1.0 if i == j else 0.0)
    factor = {}
    inverse = {}
    for i in range(5):
        for j in range(i + 1):
            running = matrix[j, i]
            for k in range(j):
                running = running - factor[i, k] * factor[j, k]
            if i == j:
                inverse[i] = 1.0 / jnp.sqrt(running)
            else:
                factor[i, j] = running * inverse[j]
    forward = []
    for i in range(5):
        running = packed[15 + i]
        for k in range(i):
            running = running - factor[i, k] * forward[k]
        forward.append(running * inverse[i])
    result = [None] * 5
    for i in reversed(range(5)):
        running = forward[i]
        for k in range(i + 1, 5):
            running = running - factor[k, i] * result[k]
        result[i] = running * inverse[i]
        out_ref[i] = result[i]


def apply_kernel(
    all_src_ref, all_extra_ref, src_low_ref, seg_low_ref, owner_ref, seg_high_ref, place_ref, idx_ref,
    mine_ref, other_ref, diag_ref, slots_ref, out_ref, update_ref, table_ref, acc_ref, slot_ref,
):
    step = pl.program_id(0)
    span = columns(step, WIDE)
    srct_ref = all_src_ref.at[:, :, span]
    extra_ref = all_extra_ref.at[:, :, span]
    fov = lax.axis_index("fov")

    @pl.when(step == 0)
    def _():
        out_ref[...] = jnp.zeros_like(out_ref)
        pieces = []
        for k in range(5):
            mine = mine_ref[k]
            other = other_ref[k]
            pieces += [mine, other]
            first = jnp.where(fov == 0, mine, other)
            second = jnp.where(fov == 0, other, mine)
            for q in range(8):
                update_ref[k : k + 1, q * 256 : (q + 1) * 256] = first[q : q + 1]
                update_ref[k : k + 1, 2048 + q * 256 : 2048 + (q + 1) * 256] = second[q : q + 1]
        stacked = jnp.concatenate(pieces, axis=0)
        table_ref[...] = jnp.concatenate(split_parts(stacked, 3), axis=1)

    idx = idx_ref[0] ^ (fov * 2048)
    high = rows_equal(16, idx >> 8)
    low = src_low_ref[:, span]
    looked = dot_nn(table_ref[...], jnp.concatenate([low] * 3, axis=0))
    chosen = [column_sum(looked[k * 16 : k * 16 + 16] * high) for k in range(5)]
    groups = []
    units = []
    for h in range(WIDE // 128):
        lanes = slice(h * 128, (h + 1) * 128)
        spread = [jnp.broadcast_to(chosen[k][:, lanes], (8, 128)) for k in range(5)]
        sums = [None] * 17
        for o in range(OBS // 8):
            rows = slice(o * 8, o * 8 + 8)
            model = srct_ref[0, rows, lanes] * spread[0]
            for k in range(1, 5):
                model = model + srct_ref[k, rows, lanes] * spread[k]
            residual = srct_ref[5, rows, lanes] - model
            phase = extra_ref[4, rows, lanes]
            moments = [extra_ref[c, rows, lanes] * residual for c in range(4)]
            terms = list(moments)
            for _ in range(3):
                moments = [m * phase for m in moments]
                terms += moments
            terms.append(extra_ref[5, rows, lanes] * residual)
            sums = terms if o == 0 else [s + t for s, t in zip(sums, terms)]
        groups.append(jnp.concatenate([fold(sums[:8]), fold(sums[8:16])], axis=0))
        units.append(column_sum(sums[16]))
    left = masked_rows(seg_high_ref[:, span], [jnp.concatenate(groups, axis=1)], 2)
    accumulate(acc_ref, repeated_dot(left, seg_low_ref[:, span], 2), step)
    left = masked_rows(place_ref[:, span], [jnp.concatenate(units, axis=1)], 2)
    accumulate(slot_ref, repeated_dot(left, owner_ref[:, span], 2), step)

    @pl.when(step == WIDE_STEPS - 1)
    def _():
        tm = lax.axis_index("tm")
        slots = jnp.concatenate([slot_ref[...], slots_ref[...], jnp.zeros((CAP, RANGES), F32)], axis=0)
        out_ref[pl.ds(0, RANGES, stride=PIECES), :] = slots.T
        first_half = lax.broadcasted_iota(jnp.int32, (16, 128), 1) < 64
        for c in range(4):
            moments = [acc_ref[(k * 4 + c) * 16 : (k * 4 + c) * 16 + 16] for k in range(4)]
            right = knots_of([spline_from_moments(moments, j) for j in range(4)])
            far = pltpu.roll(diag_ref[c], 64, 1)
            start = tm * 2 * PIECES + 1 + c
            out_ref[pl.ds(start, 16, stride=8 * PIECES), :] = jnp.where(first_half, right, far)
            out_ref[pl.ds(start + PIECES, 16, stride=8 * PIECES), :] = jnp.where(first_half, far, right)


def attitude_kernel(in_ref, att_ref):
    base = lax.axis_index("tm") * 2 * PIECES + 1
    knots = None
    for s in range(16):
        for f in range(2):
            part = in_ref[pl.ds(base + (s * 8 + f) * PIECES, 4), :]
            knots = part if knots is None else knots + part
    lower = lax.broadcasted_iota(jnp.int32, (4, 128), 1) < 64
    mine = lower == (lax.axis_index("fov") == 0)
    att_ref[...] = jnp.where(mine, knots / (1.0 + pltpu.roll(knots, 64, 1)), 0.0)


def calibration_kernel(in_ref, cal_ref, left_ref, right_ref):
    slots = in_ref[pl.ds(0, RANGES, stride=PIECES), :].T
    unit = slots[64:96].astype(jnp.int32)
    parts = wide_parts(slots[:64], 2)
    for k in range(CAP):
        lanes = slice(k * 128, (k + 1) * 128)
        inner = unit[k : k + 1]
        right_ref[:, lanes] = narrow_rows_equal(128, inner & 127)
        high = narrow_rows_equal(32, inner >> 7)
        for n in range(2):
            for v in range(2):
                row = jnp.broadcast_to(parts[n][v * 32 + k : v * 32 + k + 1], (32, 128)).astype(BF16)
                left_ref[(n * 2 + v) * 32 : (n * 2 + v + 1) * 32, lanes] = high * row
    sums = dot_nt(left_ref[...], right_ref[...])
    sums = sums[:64] + sums[64:]
    cal_ref[...] = sums[:32] / (1.0 + sums[32:])


VMEM = pl.BlockSpec(memory_space=pltpu.VMEM)
SMEM = pl.BlockSpec(memory_space=pltpu.SMEM)
ROW = pl.BlockSpec((1, 1, NB), lambda s: (s, 0, 0))
WIDE_ROW = pl.BlockSpec((1, 1, WIDE), lambda s: (s, 0, 0))


def on_chip(*arrays):
    return [pltpu.with_memory_space_constraint(a, pltpu.VMEM) for a in arrays]


def off_chip(*arrays):
    return [pltpu.with_memory_space_constraint(a, pltpu.HBM) for a in arrays]


def whole(shape):
    return pl.BlockSpec(shape, lambda s: (0,) * len(shape))


def shards(
    src_partials,
    att_partials,
    cal_partials,
    obs_phase,
    obs_residual,
    block_source,
    block_segment,
    block_unit,
    live_blocks,
):
    source = block_source.reshape(WIDE_STEPS, 1, WIDE)
    segment = block_segment.reshape(STEPS, 1, NB)
    unit = block_unit.reshape(STEPS, 1, NB)
    src = jnp.transpose(src_partials, (1, 0, 2))
    att = att_partials.reshape(BLK * 4, OBS)
    sequential = pltpu.CompilerParams(dimension_semantics=("arbitrary",), vmem_limit_bytes=24 * 1024 * 1024)
    small = pltpu.CompilerParams(vmem_limit_bytes=4 * 1024 * 1024)
    keep, send, srct, src_low = pl.pallas_call(
        normals_kernel,
        grid=(WIDE_STEPS,),
        in_specs=[
            SMEM,
            pl.BlockSpec((5, WIDE, OBS), lambda s: (0, s, 0)),
            pl.BlockSpec((WIDE, OBS), lambda s: (s, 0)),
            WIDE_ROW,
        ],
        out_specs=[VMEM] * 4,
        out_shape=[
            pltpu.VMEM((20, 8, 256), F32),
            pltpu.VMEM((20, 8, 256), F32),
            pltpu.VMEM((6, OBS, BLK), F32),
            pltpu.VMEM((256, BLK), BF16),
        ],
        scratch_shapes=[pltpu.VMEM((320, 256), F32)],
        compiler_params=sequential,
        name="normals",
    )(live_blocks, *off_chip(src, obs_residual, source))
    half = pl.pallas_call(
        join_kernel,
        in_specs=[VMEM] * 2,
        out_specs=VMEM,
        out_shape=pltpu.VMEM((20, 8, 256), F32),
        compiler_params=small,
        name="join",
    )(*on_chip(keep, lax.ppermute(send, "fov", [(0, 1), (1, 0)])))
    half, live_later = lax.optimization_barrier((half, live_blocks))
    around = [lax.ppermute(half, "tm", [(i, (i + d) % 4) for i in range(4)]) for d in (1, 2, 3)]
    extra, seg_low, owner, seg_high, place, diag_knots, diag_slots = pl.pallas_call(
        diag_kernel,
        grid=(STEPS,),
        in_specs=[
            SMEM,
            pl.BlockSpec((NB * 4, OBS), lambda s: (s, 0)),
            pl.BlockSpec((NB, OBS), lambda s: (s, 0)),
            pl.BlockSpec((NB, OBS), lambda s: (s, 0)),
            ROW,
            ROW,
        ],
        out_specs=[VMEM] * 7,
        out_shape=[
            pltpu.VMEM((6, OBS, BLK), F32),
            pltpu.VMEM((128, BLK), BF16),
            pltpu.VMEM((RANGES, BLK), BF16),
            pltpu.VMEM((16, BLK), BF16),
            pltpu.VMEM((CAP, BLK), BF16),
            pltpu.VMEM((4, 16, 128), F32),
            pltpu.VMEM((64, RANGES), F32),
        ],
        scratch_shapes=[
            pltpu.VMEM((256, 128), F32),
            pltpu.VMEM((64, RANGES), F32),
            pltpu.VMEM((RANGES, NB), F32),
        ],
        compiler_params=sequential,
        cost_estimate=pl.CostEstimate(flops=200_000_000, bytes_accessed=12_000_000, transcendentals=0),
        name="diag",
    )(live_later, att, obs_phase, cal_partials, segment, unit)
    around, diag_knots = lax.optimization_barrier((around, diag_knots))
    mine = pl.pallas_call(
        solve_kernel,
        in_specs=[VMEM] * 4,
        out_specs=VMEM,
        out_shape=pltpu.VMEM((5, 8, 256), F32),
        compiler_params=small,
        name="solve",
    )(*on_chip(half, *around))
    other = lax.ppermute(mine, "fov", [(0, 1), (1, 0)])
    outgoing, src_update = pl.pallas_call(
        apply_kernel,
        grid=(WIDE_STEPS,),
        in_specs=[VMEM] * 7 + [WIDE_ROW] + [VMEM] * 4,
        out_specs=[VMEM, whole((5, 4096))],
        out_shape=[
            pltpu.VMEM((128 * PIECES, 128), F32),
            jax.ShapeDtypeStruct((5, 4096), F32),
        ],
        scratch_shapes=[
            pltpu.VMEM((80, 768), BF16),
            pltpu.VMEM((256, 128), F32),
            pltpu.VMEM((CAP, RANGES), F32),
        ],
        compiler_params=sequential,
        name="apply",
    )(
        *on_chip(srct, extra, src_low, seg_low, owner, seg_high, place),
        source,
        *on_chip(mine, other, diag_knots, diag_slots),
    )
    arrived = lax.all_to_all(
        outgoing.reshape(128, 1, PIECES * 128), ALL, split_axis=0, concat_axis=0, tiled=True
    ).reshape(128 * PIECES, 128)
    att_half = pl.pallas_call(
        attitude_kernel,
        in_specs=[VMEM],
        out_specs=VMEM,
        out_shape=pltpu.VMEM((4, 128), F32),
        compiler_params=small,
        name="attitude",
    )(*on_chip(arrived))
    att_other = lax.ppermute(att_half, "fov", [(0, 1), (1, 0)])
    cal_update = pl.pallas_call(
        calibration_kernel,
        in_specs=[VMEM],
        out_specs=VMEM,
        out_shape=jax.ShapeDtypeStruct((32, 128), F32),
        scratch_shapes=[pltpu.VMEM((128, CAP * 128), BF16), pltpu.VMEM((128, CAP * 128), BF16)],
        cost_estimate=pl.CostEstimate(flops=100_000_000, bytes_accessed=400_000, transcendentals=0),
        name="calibration",
    )(*on_chip(arrived))
    att_update = att_half + att_other
    return (src_update, att_update.reshape(4, 1, 128), cal_update.reshape(SHARE))


def solution(mesh):
    return jax.shard_map(
        shards,
        mesh=mesh,
        in_specs=(
            P(ALL, None, None),
            P(ALL, None, None),
            P(ALL, None),
            P(ALL, None),
            P(ALL, None),
            P(ALL),
            P(ALL),
            P(ALL),
            P(ALL),
        ),
        out_specs=(P(None, "sky"), P(None, "tm", "sky"), P(ALL)),
        check_vma=False,
    )
```

```python
import jax
import jax.numpy as jnp
from jax import lax
from jax.experimental import pallas as pl
from jax.experimental.pallas import tpu as pltpu
from jax.sharding import PartitionSpec as P

BLK = 2048
CUT = 256
WIDE = 512
WIDE_STEPS = BLK // WIDE
OBS = 128
CAP = 32
RANGES = 128
SHARE = 4096
PIECES = 5
F32 = jnp.float32
BF16 = jnp.bfloat16
ALL = ("sky", "tm", "fov")

index_pairs = [(i, j) for i in range(5) for j in range(i, 5)]


def split_parts(x, count):
    parts = []
    for _ in range(count - 1):
        part = x.astype(BF16)
        parts.append(part)
        x = x - part.astype(F32)
    parts.append(x.astype(BF16))
    return parts


def dot_nt(a, b):
    return lax.dot_general(a, b, (((1,), (1,)), ((), ())), preferred_element_type=F32)


def dot_nn(a, b):
    return lax.dot_general(a, b, (((1,), (0,)), ((), ())), preferred_element_type=F32)


def rows_equal(count, row):
    iota = lax.broadcasted_iota(jnp.int32, (count, row.shape[1]), 0)
    return jnp.where(iota == row, 1.0, 0.0)


def narrow_rows_equal(count, row):
    iota = lax.broadcasted_iota(jnp.int32, (count, row.shape[1]), 0).astype(F32).astype(BF16)
    wide = jnp.broadcast_to(row.astype(F32), (count, row.shape[1])).astype(BF16)
    return jnp.where(iota == wide, jnp.ones((), BF16), jnp.zeros((), BF16))


def accumulate(ref, product, step):
    @pl.when(step == 0)
    def _():
        ref[...] = product

    @pl.when(step > 0)
    def _():
        ref[...] += product


def live_row(live_ref, step, width):
    position = step * width + lax.broadcasted_iota(jnp.int32, (1, width), 1)
    return jnp.where(position < live_ref[0], 1.0, 0.0)


def columns(step, width):
    return pl.ds(pl.multiple_of(step * width, width), width)


def row_bit(bit):
    return (lax.broadcasted_iota(jnp.int32, (8, 128), 0) & bit) == 0


def fold(accs):
    upper = row_bit(4)
    level = [
        jnp.where(upper, accs[i], accs[i + 4]) + pltpu.roll(jnp.where(upper, accs[i + 4], accs[i]), 4, 0)
        for i in range(4)
    ]
    upper = row_bit(2)
    level = [
        jnp.where(upper, level[i], level[i + 2])
        + jnp.where(upper, pltpu.roll(level[i], 6, 0), pltpu.roll(level[i + 2], 2, 0))
        for i in range(2)
    ]
    upper = row_bit(1)
    return jnp.where(upper, level[0], level[1]) + jnp.where(
        upper, pltpu.roll(level[0], 7, 0), pltpu.roll(level[1], 1, 0)
    )


def wide_parts(x, count):
    parts = []
    for _ in range(count - 1):
        part = x.astype(BF16).astype(F32)
        parts.append(part)
        x = x - part
    return parts + [x]


def masked_rows(mask, blocks, count):
    sides = []
    split = [wide_parts(block, count) for block in blocks]
    for n in range(count):
        pieces = []
        for parts in split:
            for k in range(parts[n].shape[0]):
                pieces.append(mask * jnp.broadcast_to(parts[n][k : k + 1], mask.shape).astype(BF16))
        sides.append(jnp.concatenate(pieces, axis=0))
    return jnp.concatenate(sides, axis=1)


def repeated_dot(left, right, count):
    return dot_nt(left, jnp.concatenate([right] * count, axis=1))


def column_sum(x):
    return jnp.sum(x, axis=0, keepdims=True)


def spline_basis(phase):
    rest = 1.0 - phase
    square = phase * phase
    cubed = square * phase
    half = 0.5 * cubed
    return (
        rest * rest * rest * (1.0 / 6.0),
        half - square + (2.0 / 3.0),
        0.5 * (square + phase) - half + (1.0 / 6.0),
        cubed * (1.0 / 6.0),
    )


def spline_from_moments(m, j):
    sixth = 1.0 / 6.0
    if j == 0:
        return (m[0] - m[3]) * sixth + 0.5 * (m[2] - m[1])
    if j == 1:
        return m[0] * (2.0 / 3.0) - m[2] + 0.5 * m[3]
    if j == 2:
        return m[0] * sixth + 0.5 * (m[1] + m[2] - m[3])
    return m[3] * sixth


def normals_kernel(live_ref, src_ref, res_ref, idx_ref, keep_ref, send_ref, all_src_ref, all_low_ref, acc_ref):
    step = pl.program_id(0)
    span = columns(step, WIDE)
    srct_ref = all_src_ref.at[:, :, span]
    idx = idx_ref[0] ^ (lax.axis_index("fov") * 2048)
    high = (rows_equal(16, idx >> 8) * live_row(live_ref, step, WIDE)).astype(BF16)
    low = narrow_rows_equal(256, idx & 255)
    all_low_ref[:, span] = low
    groups = []
    spare = []
    for h in range(WIDE // 128):
        lanes = slice(h * 128, (h + 1) * 128)
        for i in range(5):
            srct_ref[i, :, lanes] = src_ref[i, lanes, :].T
        srct_ref[5, :, lanes] = res_ref[lanes, :].T
        sums = [None] * 20
        for o in range(OBS // 8):
            rows = [srct_ref[i, o * 8 : o * 8 + 8, lanes] for i in range(6)]
            terms = [rows[i] * rows[j] for i, j in index_pairs] + [rows[i] * rows[5] for i in range(5)]
            sums = terms if o == 0 else [s + t for s, t in zip(sums, terms)]
        groups.append(jnp.concatenate([fold(sums[:8]), fold(sums[8:16])], axis=0))
        spare.append(sums[16:])
    rest = []
    for h in range(0, WIDE // 128, 2):
        both = fold(spare[h] + spare[h + 1])
        rest += [both[:4], both[4:]]
    blocks = [jnp.concatenate(groups, axis=1), jnp.concatenate(rest, axis=1)]
    accumulate(acc_ref, repeated_dot(masked_rows(high, blocks, 3), low, 3), step)

    @pl.when(step == WIDE_STEPS - 1)
    def _():
        for k in range(20):
            keep_ref[k] = acc_ref[k * 16 : k * 16 + 8]
            send_ref[k] = acc_ref[k * 16 + 8 : k * 16 + 16]


def shifted(rows, distance):
    moved = pltpu.roll(rows, distance, 1)
    below = pltpu.roll(moved, 1, 0)
    row = lax.broadcasted_iota(jnp.int32, rows.shape, 0)
    lane = lax.broadcasted_iota(jnp.int32, rows.shape, 1)
    return jnp.where(lane >= distance, moved, jnp.where(row > 0, below, 0.0))


def knots_of(parts):
    total = parts[0]
    for j in range(1, 4):
        total = total + shifted(parts[j], j)
    return total


def diag_kernel(
    live_ref, att_ref, pha_ref, cal_ref, seg_ref, unit_ref,
    all_extra_ref, all_low_ref, all_owner_ref, all_high_ref, all_place_ref, knots_ref, slots_ref,
    acc_ref, slot_ref, carry_ref,
):
    step = pl.program_id(0)
    span = columns(step, WIDE)
    extra_ref = all_extra_ref.at[:, :, span]
    live = live_row(live_ref, step, WIDE)
    unit = unit_ref[0]
    owner = rows_equal(RANGES, unit >> 12)
    owner_low = owner.astype(BF16)
    all_owner_ref[:, span] = owner_low
    before = lax.broadcasted_iota(jnp.int32, (CUT, CUT), 0) < lax.broadcasted_iota(jnp.int32, (CUT, CUT), 1)
    before = jnp.where(before, 1.0, 0.0).astype(BF16)
    carry = jnp.where(step > 0, carry_ref[...], 0.0)
    ranks = []
    for h in range(WIDE // CUT):
        part = slice(h * CUT, (h + 1) * CUT)
        earlier = dot_nn(owner_low[:, part], before) + carry
        ranks.append(column_sum(owner[:, part] * earlier))
        carry = carry + dot_nn(owner_low[:, part], jnp.ones((CUT, CUT), BF16))
    carry_ref[...] = carry
    rank = jnp.concatenate(ranks, axis=1).astype(jnp.int32)
    place = rows_equal(CAP, rank)
    place_live = (place * live).astype(BF16)
    all_place_ref[:, span] = place_live
    seg = seg_ref[0]
    seg_high = (rows_equal(16, seg >> 7) * live).astype(BF16)
    seg_low = narrow_rows_equal(128, seg & 127)
    all_high_ref[:, span] = seg_high
    all_low_ref[:, span] = seg_low
    groups = []
    units = []
    for h in range(WIDE // 128):
        lanes = slice(h * 128, (h + 1) * 128)
        for c in range(4):
            extra_ref[c, :, lanes] = att_ref[pl.ds(h * 512 + c, 128, stride=4), :].T
        extra_ref[4, :, lanes] = pha_ref[lanes, :].T
        extra_ref[5, :, lanes] = cal_ref[lanes, :].T
        sums = [None] * 17
        for o in range(OBS // 8):
            rows = [extra_ref[i, o * 8 : o * 8 + 8, lanes] for i in range(6)]
            basis = [b * b for b in spline_basis(rows[4])]
            squares = [rows[c] * rows[c] for c in range(4)]
            terms = [b * s for b in basis for s in squares] + [rows[5] * rows[5]]
            sums = terms if o == 0 else [s + t for s, t in zip(sums, terms)]
        groups.append(jnp.concatenate([fold(sums[:8]), fold(sums[8:16])], axis=0))
        units.append(column_sum(sums[16]))
    left = masked_rows(seg_high, [jnp.concatenate(groups, axis=1)], 2)
    accumulate(acc_ref, repeated_dot(left, seg_low, 2), step)
    inner = (unit & (SHARE - 1)).astype(F32)
    left = jnp.concatenate(
        [
            masked_rows(place_live, [jnp.concatenate(units, axis=1)], 2),
            masked_rows(place.astype(BF16), [inner], 2),
        ],
        axis=0,
    )
    accumulate(slot_ref, repeated_dot(left, owner_low, 2), step)

    @pl.when(step == WIDE_STEPS - 1)
    def _():
        for c in range(4):
            knots_ref[c] = knots_of([acc_ref[(j * 4 + c) * 16 : (j * 4 + c) * 16 + 16] for j in range(4)])
        slots_ref[...] = slot_ref[...]


def join_kernel(a_ref, b_ref, out_ref):
    out_ref[...] = a_ref[...] + b_ref[...]


def solve_kernel(a_ref, b_ref, c_ref, d_ref, out_ref):
    packed = [(a_ref[k] + c_ref[k]) + (b_ref[k] + d_ref[k]) for k in range(20)]
    matrix = {}
    for position, (i, j) in enumerate(index_pairs):
        matrix[i, j] = packed[position] + (1.0 if i == j else 0.0)
    factor = {}
    inverse = {}
    for i in range(5):
        for j in range(i + 1):
            running = matrix[j, i]
            for k in range(j):
                running = running - factor[i, k] * factor[j, k]
            if i == j:
                inverse[i] = 1.0 / jnp.sqrt(running)
            else:
                factor[i, j] = running * inverse[j]
    forward = []
    for i in range(5):
        running = packed[15 + i]
        for k in range(i):
            running = running - factor[i, k] * forward[k]
        forward.append(running * inverse[i])
    result = [None] * 5
    for i in reversed(range(5)):
        running = forward[i]
        for k in range(i + 1, 5):
            running = running - factor[k, i] * result[k]
        result[i] = running * inverse[i]
        out_ref[i] = result[i]


def apply_kernel(
    all_src_ref, all_extra_ref, src_low_ref, seg_low_ref, owner_ref, seg_high_ref, place_ref, idx_ref,
    mine_ref, other_ref, diag_ref, slots_ref, out_ref, update_ref, table_ref, acc_ref, slot_ref,
):
    step = pl.program_id(0)
    span = columns(step, WIDE)
    srct_ref = all_src_ref.at[:, :, span]
    extra_ref = all_extra_ref.at[:, :, span]
    fov = lax.axis_index("fov")

    @pl.when(step == 0)
    def _():
        out_ref[...] = jnp.zeros_like(out_ref)
        pieces = []
        for k in range(5):
            mine = mine_ref[k]
            other = other_ref[k]
            pieces += [mine, other]
            first = jnp.where(fov == 0, mine, other)
            second = jnp.where(fov == 0, other, mine)
            for q in range(8):
                update_ref[k : k + 1, q * 256 : (q + 1) * 256] = first[q : q + 1]
                update_ref[k : k + 1, 2048 + q * 256 : 2048 + (q + 1) * 256] = second[q : q + 1]
        stacked = jnp.concatenate(pieces, axis=0)
        table_ref[...] = jnp.concatenate(split_parts(stacked, 3), axis=1)

    idx = idx_ref[0] ^ (fov * 2048)
    high = rows_equal(16, idx >> 8)
    low = src_low_ref[:, span]
    looked = dot_nn(table_ref[...], jnp.concatenate([low] * 3, axis=0))
    chosen = [column_sum(looked[k * 16 : k * 16 + 16] * high) for k in range(5)]
    groups = []
    units = []
    for h in range(WIDE // 128):
        lanes = slice(h * 128, (h + 1) * 128)
        spread = [jnp.broadcast_to(chosen[k][:, lanes], (8, 128)) for k in range(5)]
        sums = [None] * 17
        for o in range(OBS // 8):
            rows = slice(o * 8, o * 8 + 8)
            model = srct_ref[0, rows, lanes] * spread[0]
            for k in range(1, 5):
                model = model + srct_ref[k, rows, lanes] * spread[k]
            residual = srct_ref[5, rows, lanes] - model
            phase = extra_ref[4, rows, lanes]
            moments = [extra_ref[c, rows, lanes] * residual for c in range(4)]
            terms = list(moments)
            for _ in range(3):
                moments = [m * phase for m in moments]
                terms += moments
            terms.append(extra_ref[5, rows, lanes] * residual)
            sums = terms if o == 0 else [s + t for s, t in zip(sums, terms)]
        groups.append(jnp.concatenate([fold(sums[:8]), fold(sums[8:16])], axis=0))
        units.append(column_sum(sums[16]))
    left = masked_rows(seg_high_ref[:, span], [jnp.concatenate(groups, axis=1)], 2)
    accumulate(acc_ref, repeated_dot(left, seg_low_ref[:, span], 2), step)
    left = masked_rows(place_ref[:, span], [jnp.concatenate(units, axis=1)], 2)
    accumulate(slot_ref, repeated_dot(left, owner_ref[:, span], 2), step)

    @pl.when(step == WIDE_STEPS - 1)
    def _():
        tm = lax.axis_index("tm")
        slots = jnp.concatenate([slot_ref[...], slots_ref[...], jnp.zeros((CAP, RANGES), F32)], axis=0)
        out_ref[pl.ds(0, RANGES, stride=PIECES), :] = slots.T
        first_half = lax.broadcasted_iota(jnp.int32, (16, 128), 1) < 64
        for c in range(4):
            moments = [acc_ref[(k * 4 + c) * 16 : (k * 4 + c) * 16 + 16] for k in range(4)]
            right = knots_of([spline_from_moments(moments, j) for j in range(4)])
            far = pltpu.roll(diag_ref[c], 64, 1)
            start = tm * 2 * PIECES + 1 + c
            out_ref[pl.ds(start, 16, stride=8 * PIECES), :] = jnp.where(first_half, right, far)
            out_ref[pl.ds(start + PIECES, 16, stride=8 * PIECES), :] = jnp.where(first_half, far, right)


def attitude_kernel(in_ref, att_ref):
    base = lax.axis_index("tm") * 2 * PIECES + 1
    knots = None
    for s in range(16):
        for f in range(2):
            part = in_ref[pl.ds(base + (s * 8 + f) * PIECES, 4), :]
            knots = part if knots is None else knots + part
    lower = lax.broadcasted_iota(jnp.int32, (4, 128), 1) < 64
    mine = lower == (lax.axis_index("fov") == 0)
    att_ref[...] = jnp.where(mine, knots / (1.0 + pltpu.roll(knots, 64, 1)), 0.0)


def calibration_kernel(in_ref, cal_ref, left_ref, right_ref):
    slots = in_ref[pl.ds(0, RANGES, stride=PIECES), :].T
    unit = slots[64:96].astype(jnp.int32)
    parts = wide_parts(slots[:64], 2)
    for k in range(CAP):
        lanes = slice(k * 128, (k + 1) * 128)
        inner = unit[k : k + 1]
        right_ref[:, lanes] = narrow_rows_equal(128, inner & 127)
        high = narrow_rows_equal(32, inner >> 7)
        for n in range(2):
            for v in range(2):
                row = jnp.broadcast_to(parts[n][v * 32 + k : v * 32 + k + 1], (32, 128)).astype(BF16)
                left_ref[(n * 2 + v) * 32 : (n * 2 + v + 1) * 32, lanes] = high * row
    sums = dot_nt(left_ref[...], right_ref[...])
    sums = sums[:64] + sums[64:]
    cal_ref[...] = sums[:32] / (1.0 + sums[32:])


VMEM = pl.BlockSpec(memory_space=pltpu.VMEM)
SMEM = pl.BlockSpec(memory_space=pltpu.SMEM)
WIDE_ROW = pl.BlockSpec((1, 1, WIDE), lambda s: (s, 0, 0))


def on_chip(*arrays):
    return [pltpu.with_memory_space_constraint(a, pltpu.VMEM) for a in arrays]


def off_chip(*arrays):
    return [pltpu.with_memory_space_constraint(a, pltpu.HBM) for a in arrays]


def whole(shape):
    return pl.BlockSpec(shape, lambda s: (0,) * len(shape))


def shards(
    src_partials,
    att_partials,
    cal_partials,
    obs_phase,
    obs_residual,
    block_source,
    block_segment,
    block_unit,
    live_blocks,
):
    source = block_source.reshape(WIDE_STEPS, 1, WIDE)
    segment = block_segment.reshape(WIDE_STEPS, 1, WIDE)
    unit = block_unit.reshape(WIDE_STEPS, 1, WIDE)
    src = jnp.transpose(src_partials, (1, 0, 2))
    att = att_partials.reshape(BLK * 4, OBS)
    sequential = pltpu.CompilerParams(dimension_semantics=("arbitrary",), vmem_limit_bytes=24 * 1024 * 1024)
    small = pltpu.CompilerParams(vmem_limit_bytes=4 * 1024 * 1024)
    keep, send, srct, src_low = pl.pallas_call(
        normals_kernel,
        grid=(WIDE_STEPS,),
        in_specs=[
            SMEM,
            pl.BlockSpec((5, WIDE, OBS), lambda s: (0, s, 0)),
            pl.BlockSpec((WIDE, OBS), lambda s: (s, 0)),
            WIDE_ROW,
        ],
        out_specs=[VMEM] * 4,
        out_shape=[
            pltpu.VMEM((20, 8, 256), F32),
            pltpu.VMEM((20, 8, 256), F32),
            pltpu.VMEM((6, OBS, BLK), F32),
            pltpu.VMEM((256, BLK), BF16),
        ],
        scratch_shapes=[pltpu.VMEM((320, 256), F32)],
        compiler_params=sequential,
        name="normals",
    )(live_blocks, *off_chip(src, obs_residual, source))
    half = pl.pallas_call(
        join_kernel,
        in_specs=[VMEM] * 2,
        out_specs=VMEM,
        out_shape=pltpu.VMEM((20, 8, 256), F32),
        compiler_params=small,
        name="join",
    )(*on_chip(keep, lax.ppermute(send, "fov", [(0, 1), (1, 0)])))
    half, live_later = lax.optimization_barrier((half, live_blocks))
    around = [lax.ppermute(half, "tm", [(i, i ^ d) for i in range(4)]) for d in (1, 2, 3)]
    extra, seg_low, owner, seg_high, place, diag_knots, diag_slots = pl.pallas_call(
        diag_kernel,
        grid=(WIDE_STEPS,),
        in_specs=[
            SMEM,
            pl.BlockSpec((WIDE * 4, OBS), lambda s: (s, 0)),
            pl.BlockSpec((WIDE, OBS), lambda s: (s, 0)),
            pl.BlockSpec((WIDE, OBS), lambda s: (s, 0)),
            WIDE_ROW,
            WIDE_ROW,
        ],
        out_specs=[VMEM] * 7,
        out_shape=[
            pltpu.VMEM((6, OBS, BLK), F32),
            pltpu.VMEM((128, BLK), BF16),
            pltpu.VMEM((RANGES, BLK), BF16),
            pltpu.VMEM((16, BLK), BF16),
            pltpu.VMEM((CAP, BLK), BF16),
            pltpu.VMEM((4, 16, 128), F32),
            pltpu.VMEM((64, RANGES), F32),
        ],
        scratch_shapes=[
            pltpu.VMEM((256, 128), F32),
            pltpu.VMEM((64, RANGES), F32),
            pltpu.VMEM((RANGES, CUT), F32),
        ],
        compiler_params=sequential,
        cost_estimate=pl.CostEstimate(flops=200_000_000, bytes_accessed=12_000_000, transcendentals=0),
        name="diag",
    )(live_later, att, obs_phase, cal_partials, segment, unit)
    around, diag_knots = lax.optimization_barrier((around, diag_knots))
    mine = pl.pallas_call(
        solve_kernel,
        in_specs=[VMEM] * 4,
        out_specs=VMEM,
        out_shape=pltpu.VMEM((5, 8, 256), F32),
        compiler_params=small,
        name="solve",
    )(*on_chip(half, *around))
    other = lax.ppermute(mine, "fov", [(0, 1), (1, 0)])
    outgoing, src_update = pl.pallas_call(
        apply_kernel,
        grid=(WIDE_STEPS,),
        in_specs=[VMEM] * 7 + [WIDE_ROW] + [VMEM] * 4,
        out_specs=[VMEM, whole((5, 4096))],
        out_shape=[
            pltpu.VMEM((128 * PIECES, 128), F32),
            jax.ShapeDtypeStruct((5, 4096), F32),
        ],
        scratch_shapes=[
            pltpu.VMEM((80, 768), BF16),
            pltpu.VMEM((256, 128), F32),
            pltpu.VMEM((CAP, RANGES), F32),
        ],
        compiler_params=sequential,
        name="apply",
    )(
        *on_chip(srct, extra, src_low, seg_low, owner, seg_high, place),
        source,
        *on_chip(mine, other, diag_knots, diag_slots),
    )
    arrived = lax.all_to_all(
        outgoing.reshape(128, 1, PIECES * 128), ALL, split_axis=0, concat_axis=0, tiled=True
    ).reshape(128 * PIECES, 128)
    att_half = pl.pallas_call(
        attitude_kernel,
        in_specs=[VMEM],
        out_specs=VMEM,
        out_shape=pltpu.VMEM((4, 128), F32),
        compiler_params=small,
        name="attitude",
    )(*on_chip(arrived))
    att_other = lax.ppermute(att_half, "fov", [(0, 1), (1, 0)])
    cal_update = pl.pallas_call(
        calibration_kernel,
        in_specs=[VMEM],
        out_specs=VMEM,
        out_shape=jax.ShapeDtypeStruct((32, 128), F32),
        scratch_shapes=[pltpu.VMEM((128, CAP * 128), BF16), pltpu.VMEM((128, CAP * 128), BF16)],
        cost_estimate=pl.CostEstimate(flops=100_000_000, bytes_accessed=400_000, transcendentals=0),
        name="calibration",
    )(*on_chip(arrived))
    att_update = att_half + att_other
    return (src_update, att_update.reshape(4, 1, 128), cal_update.reshape(SHARE))


def solution(mesh):
    return jax.shard_map(
        shards,
        mesh=mesh,
        in_specs=(
            P(ALL, None, None),
            P(ALL, None, None),
            P(ALL, None),
            P(ALL, None),
            P(ALL, None),
            P(ALL),
            P(ALL),
            P(ALL),
            P(ALL),
        ),
        out_specs=(P(None, "sky"), P(None, "tm", "sky"), P(ALL)),
        check_vma=False,
    )
```

```python
import jax
import jax.numpy as jnp
from jax import lax
from jax.experimental import pallas as pl
from jax.experimental.pallas import tpu as pltpu
from jax.sharding import PartitionSpec as P

BLK = 2048
CUT = 256
WIDE = 512
WIDE_STEPS = BLK // WIDE
LONG = 1024
LONG_STEPS = BLK // LONG
OBS = 128
CAP = 32
RANGES = 128
SHARE = 4096
PIECES = 5
F32 = jnp.float32
BF16 = jnp.bfloat16
ALL = ("sky", "tm", "fov")

index_pairs = [(i, j) for i in range(5) for j in range(i, 5)]


def split_parts(x, count):
    parts = []
    for _ in range(count - 1):
        part = x.astype(BF16)
        parts.append(part)
        x = x - part.astype(F32)
    parts.append(x.astype(BF16))
    return parts


def dot_nt(a, b):
    return lax.dot_general(a, b, (((1,), (1,)), ((), ())), preferred_element_type=F32)


def dot_nn(a, b):
    return lax.dot_general(a, b, (((1,), (0,)), ((), ())), preferred_element_type=F32)


def rows_equal(count, row):
    iota = lax.broadcasted_iota(jnp.int32, (count, row.shape[1]), 0)
    return jnp.where(iota == row, 1.0, 0.0)


def narrow_rows_equal(count, row):
    iota = lax.broadcasted_iota(jnp.int32, (count, row.shape[1]), 0).astype(F32).astype(BF16)
    wide = jnp.broadcast_to(row.astype(F32), (count, row.shape[1])).astype(BF16)
    return jnp.where(iota == wide, jnp.ones((), BF16), jnp.zeros((), BF16))


def accumulate(ref, product, step):
    @pl.when(step == 0)
    def _():
        ref[...] = product

    @pl.when(step > 0)
    def _():
        ref[...] += product


def live_row(live_ref, step, width):
    position = step * width + lax.broadcasted_iota(jnp.int32, (1, width), 1)
    return jnp.where(position < live_ref[0], 1.0, 0.0)


def columns(step, width):
    return pl.ds(pl.multiple_of(step * width, width), width)


def row_bit(bit):
    return (lax.broadcasted_iota(jnp.int32, (8, 128), 0) & bit) == 0


def fold(accs):
    upper = row_bit(4)
    level = [
        jnp.where(upper, accs[i], accs[i + 4]) + pltpu.roll(jnp.where(upper, accs[i + 4], accs[i]), 4, 0)
        for i in range(4)
    ]
    upper = row_bit(2)
    level = [
        jnp.where(upper, level[i], level[i + 2])
        + jnp.where(upper, pltpu.roll(level[i], 6, 0), pltpu.roll(level[i + 2], 2, 0))
        for i in range(2)
    ]
    upper = row_bit(1)
    return jnp.where(upper, level[0], level[1]) + jnp.where(
        upper, pltpu.roll(level[0], 7, 0), pltpu.roll(level[1], 1, 0)
    )


def wide_parts(x, count):
    parts = []
    for _ in range(count - 1):
        part = x.astype(BF16).astype(F32)
        parts.append(part)
        x = x - part
    return parts + [x]


def masked_rows(mask, blocks, count):
    sides = []
    split = [wide_parts(block, count) for block in blocks]
    for n in range(count):
        pieces = []
        for parts in split:
            for k in range(parts[n].shape[0]):
                pieces.append(mask * jnp.broadcast_to(parts[n][k : k + 1], mask.shape).astype(BF16))
        sides.append(jnp.concatenate(pieces, axis=0))
    return jnp.concatenate(sides, axis=1)


def repeated_dot(left, right, count):
    return dot_nt(left, jnp.concatenate([right] * count, axis=1))


def column_sum(x):
    return jnp.sum(x, axis=0, keepdims=True)


def spline_basis(phase):
    rest = 1.0 - phase
    square = phase * phase
    cubed = square * phase
    half = 0.5 * cubed
    return (
        rest * rest * rest * (1.0 / 6.0),
        half - square + (2.0 / 3.0),
        0.5 * (square + phase) - half + (1.0 / 6.0),
        cubed * (1.0 / 6.0),
    )


def spline_from_moments(m, j):
    sixth = 1.0 / 6.0
    if j == 0:
        return (m[0] - m[3]) * sixth + 0.5 * (m[2] - m[1])
    if j == 1:
        return m[0] * (2.0 / 3.0) - m[2] + 0.5 * m[3]
    if j == 2:
        return m[0] * sixth + 0.5 * (m[1] + m[2] - m[3])
    return m[3] * sixth


def normals_kernel(live_ref, src_ref, res_ref, idx_ref, keep_ref, send_ref, all_src_ref, all_low_ref, acc_ref):
    step = pl.program_id(0)
    span = columns(step, WIDE)
    srct_ref = all_src_ref.at[:, :, span]
    idx = idx_ref[0] ^ (lax.axis_index("fov") * 2048)
    live = live_row(live_ref, step, WIDE)
    total = None
    for part in range(WIDE // CUT):
        cut = slice(part * CUT, (part + 1) * CUT)
        high = (rows_equal(16, idx[:, cut] >> 8) * live[:, cut]).astype(BF16)
        low = narrow_rows_equal(256, idx[:, cut] & 255)
        all_low_ref[:, columns(step * (WIDE // CUT) + part, CUT)] = low
        groups = []
        spare = []
        for h in range(CUT // 128):
            lanes = slice(part * CUT + h * 128, part * CUT + (h + 1) * 128)
            for i in range(5):
                srct_ref[i, :, lanes] = src_ref[i, lanes, :].T
            srct_ref[5, :, lanes] = res_ref[lanes, :].T
            sums = [None] * 20
            for o in range(OBS // 8):
                rows = [srct_ref[i, o * 8 : o * 8 + 8, lanes] for i in range(6)]
                terms = [rows[i] * rows[j] for i, j in index_pairs] + [rows[i] * rows[5] for i in range(5)]
                sums = terms if o == 0 else [s + t for s, t in zip(sums, terms)]
            groups.append(jnp.concatenate([fold(sums[:8]), fold(sums[8:16])], axis=0))
            spare.append(sums[16:])
        both = fold(spare[0] + spare[1])
        blocks = [jnp.concatenate(groups, axis=1), jnp.concatenate([both[:4], both[4:]], axis=1)]
        product = repeated_dot(masked_rows(high, blocks, 3), low, 3)
        total = product if part == 0 else total + product
    accumulate(acc_ref, total, step)

    @pl.when(step == WIDE_STEPS - 1)
    def _():
        for k in range(20):
            keep_ref[k] = acc_ref[k * 16 : k * 16 + 8]
            send_ref[k] = acc_ref[k * 16 + 8 : k * 16 + 16]


def shifted(rows, distance):
    moved = pltpu.roll(rows, distance, 1)
    below = pltpu.roll(moved, 1, 0)
    row = lax.broadcasted_iota(jnp.int32, rows.shape, 0)
    lane = lax.broadcasted_iota(jnp.int32, rows.shape, 1)
    return jnp.where(lane >= distance, moved, jnp.where(row > 0, below, 0.0))


def knots_of(parts):
    total = parts[0]
    for j in range(1, 4):
        total = total + shifted(parts[j], j)
    return total


def diag_kernel(
    live_ref, att_ref, pha_ref, cal_ref, seg_ref, unit_ref,
    all_extra_ref, all_low_ref, all_owner_ref, all_high_ref, all_place_ref, knots_ref, slots_ref,
    acc_ref, slot_ref, carry_ref,
):
    step = pl.program_id(0)
    span = columns(step, WIDE)
    extra_ref = all_extra_ref.at[:, :, span]
    live = live_row(live_ref, step, WIDE)
    unit = unit_ref[0]
    owner = rows_equal(RANGES, unit >> 12)
    owner_low = owner.astype(BF16)
    all_owner_ref[:, span] = owner_low
    before = lax.broadcasted_iota(jnp.int32, (CUT, CUT), 0) < lax.broadcasted_iota(jnp.int32, (CUT, CUT), 1)
    before = jnp.where(before, 1.0, 0.0).astype(BF16)
    carry = jnp.where(step > 0, carry_ref[...], 0.0)
    ranks = []
    for h in range(WIDE // CUT):
        part = slice(h * CUT, (h + 1) * CUT)
        earlier = dot_nn(owner_low[:, part], before) + carry
        ranks.append(column_sum(owner[:, part] * earlier))
        carry = carry + dot_nn(owner_low[:, part], jnp.ones((CUT, CUT), BF16))
    carry_ref[...] = carry
    rank = jnp.concatenate(ranks, axis=1).astype(jnp.int32)
    place = rows_equal(CAP, rank)
    place_live = (place * live).astype(BF16)
    all_place_ref[:, span] = place_live
    seg = seg_ref[0]
    seg_high = (rows_equal(16, seg >> 7) * live).astype(BF16)
    seg_low = narrow_rows_equal(128, seg & 127)
    all_high_ref[:, span] = seg_high
    all_low_ref[:, span] = seg_low
    groups = []
    units = []
    for h in range(WIDE // 128):
        lanes = slice(h * 128, (h + 1) * 128)
        for c in range(4):
            extra_ref[c, :, lanes] = att_ref[pl.ds(h * 512 + c, 128, stride=4), :].T
        extra_ref[4, :, lanes] = pha_ref[lanes, :].T
        extra_ref[5, :, lanes] = cal_ref[lanes, :].T
        sums = [None] * 17
        for o in range(OBS // 8):
            rows = [extra_ref[i, o * 8 : o * 8 + 8, lanes] for i in range(6)]
            basis = [b * b for b in spline_basis(rows[4])]
            squares = [rows[c] * rows[c] for c in range(4)]
            terms = [b * s for b in basis for s in squares] + [rows[5] * rows[5]]
            sums = terms if o == 0 else [s + t for s, t in zip(sums, terms)]
        groups.append(jnp.concatenate([fold(sums[:8]), fold(sums[8:16])], axis=0))
        units.append(column_sum(sums[16]))
    left = masked_rows(seg_high, [jnp.concatenate(groups, axis=1)], 2)
    accumulate(acc_ref, repeated_dot(left, seg_low, 2), step)
    inner = (unit & (SHARE - 1)).astype(F32)
    left = jnp.concatenate(
        [
            masked_rows(place_live, [jnp.concatenate(units, axis=1)], 2),
            masked_rows(place.astype(BF16), [inner], 2),
        ],
        axis=0,
    )
    accumulate(slot_ref, repeated_dot(left, owner_low, 2), step)

    @pl.when(step == WIDE_STEPS - 1)
    def _():
        for c in range(4):
            knots_ref[c] = knots_of([acc_ref[(j * 4 + c) * 16 : (j * 4 + c) * 16 + 16] for j in range(4)])
        slots_ref[...] = slot_ref[...]


def join_kernel(a_ref, b_ref, out_ref):
    out_ref[...] = a_ref[...] + b_ref[...]


def solve_kernel(a_ref, b_ref, c_ref, d_ref, out_ref):
    packed = [(a_ref[k] + c_ref[k]) + (b_ref[k] + d_ref[k]) for k in range(20)]
    matrix = {}
    for position, (i, j) in enumerate(index_pairs):
        matrix[i, j] = packed[position] + (1.0 if i == j else 0.0)
    factor = {}
    inverse = {}
    for i in range(5):
        for j in range(i + 1):
            running = matrix[j, i]
            for k in range(j):
                running = running - factor[i, k] * factor[j, k]
            if i == j:
                inverse[i] = 1.0 / jnp.sqrt(running)
            else:
                factor[i, j] = running * inverse[j]
    forward = []
    for i in range(5):
        running = packed[15 + i]
        for k in range(i):
            running = running - factor[i, k] * forward[k]
        forward.append(running * inverse[i])
    result = [None] * 5
    for i in reversed(range(5)):
        running = forward[i]
        for k in range(i + 1, 5):
            running = running - factor[k, i] * result[k]
        result[i] = running * inverse[i]
        out_ref[i] = result[i]


def apply_kernel(
    all_src_ref, all_extra_ref, src_low_ref, seg_low_ref, owner_ref, seg_high_ref, place_ref, idx_ref,
    mine_ref, other_ref, diag_ref, slots_ref, out_ref, update_ref, table_ref, acc_ref, slot_ref,
):
    step = pl.program_id(0)
    span = columns(step, LONG)
    srct_ref = all_src_ref.at[:, :, span]
    extra_ref = all_extra_ref.at[:, :, span]
    fov = lax.axis_index("fov")

    @pl.when(step == 0)
    def _():
        out_ref[...] = jnp.zeros_like(out_ref)
        pieces = []
        for k in range(5):
            mine = mine_ref[k]
            other = other_ref[k]
            pieces += [mine, other]
            first = jnp.where(fov == 0, mine, other)
            second = jnp.where(fov == 0, other, mine)
            for q in range(8):
                update_ref[k : k + 1, q * 256 : (q + 1) * 256] = first[q : q + 1]
                update_ref[k : k + 1, 2048 + q * 256 : 2048 + (q + 1) * 256] = second[q : q + 1]
        stacked = jnp.concatenate(pieces, axis=0)
        table_ref[...] = jnp.concatenate(split_parts(stacked, 3), axis=0)

    idx = idx_ref[0] ^ (fov * 2048)
    knot_sums = None
    slot_sums = None
    for part in range(LONG // CUT):
        cut = slice(part * CUT, (part + 1) * CUT)
        place = columns(step * (LONG // CUT) + part, CUT)
        high = rows_equal(16, idx[:, cut] >> 8)
        looked = dot_nn(table_ref[...], src_low_ref[:, place])
        looked = looked[:80] + looked[80:160] + looked[160:]
        chosen = [column_sum(looked[k * 16 : k * 16 + 16] * high) for k in range(5)]
        groups = []
        units = []
        for h in range(CUT // 128):
            lanes = slice(part * CUT + h * 128, part * CUT + (h + 1) * 128)
            spread = [jnp.broadcast_to(chosen[k][:, h * 128 : (h + 1) * 128], (8, 128)) for k in range(5)]
            sums = [None] * 17
            for o in range(OBS // 8):
                rows = slice(o * 8, o * 8 + 8)
                model = srct_ref[0, rows, lanes] * spread[0]
                for k in range(1, 5):
                    model = model + srct_ref[k, rows, lanes] * spread[k]
                residual = srct_ref[5, rows, lanes] - model
                phase = extra_ref[4, rows, lanes]
                moments = [extra_ref[c, rows, lanes] * residual for c in range(4)]
                terms = list(moments)
                for _ in range(3):
                    moments = [m * phase for m in moments]
                    terms += moments
                terms.append(extra_ref[5, rows, lanes] * residual)
                sums = terms if o == 0 else [s + t for s, t in zip(sums, terms)]
            groups.append(jnp.concatenate([fold(sums[:8]), fold(sums[8:16])], axis=0))
            units.append(column_sum(sums[16]))
        left = masked_rows(seg_high_ref[:, place], [jnp.concatenate(groups, axis=1)], 2)
        knot_part = repeated_dot(left, seg_low_ref[:, place], 2)
        left = masked_rows(place_ref[:, place], [jnp.concatenate(units, axis=1)], 2)
        slot_part = repeated_dot(left, owner_ref[:, place], 2)
        knot_sums = knot_part if part == 0 else knot_sums + knot_part
        slot_sums = slot_part if part == 0 else slot_sums + slot_part
    accumulate(acc_ref, knot_sums, step)
    accumulate(slot_ref, slot_sums, step)

    @pl.when(step == LONG_STEPS - 1)
    def _():
        tm = lax.axis_index("tm")
        slots = jnp.concatenate([slot_ref[...], slots_ref[...], jnp.zeros((CAP, RANGES), F32)], axis=0)
        out_ref[pl.ds(0, RANGES, stride=PIECES), :] = slots.T
        first_half = lax.broadcasted_iota(jnp.int32, (16, 128), 1) < 64
        for c in range(4):
            moments = [acc_ref[(k * 4 + c) * 16 : (k * 4 + c) * 16 + 16] for k in range(4)]
            right = knots_of([spline_from_moments(moments, j) for j in range(4)])
            far = pltpu.roll(diag_ref[c], 64, 1)
            start = tm * 2 * PIECES + 1 + c
            out_ref[pl.ds(start, 16, stride=8 * PIECES), :] = jnp.where(first_half, right, far)
            out_ref[pl.ds(start + PIECES, 16, stride=8 * PIECES), :] = jnp.where(first_half, far, right)


def attitude_kernel(in_ref, att_ref):
    base = lax.axis_index("tm") * 2 * PIECES + 1
    knots = None
    for s in range(16):
        for f in range(2):
            part = in_ref[pl.ds(base + (s * 8 + f) * PIECES, 4), :]
            knots = part if knots is None else knots + part
    lower = lax.broadcasted_iota(jnp.int32, (4, 128), 1) < 64
    mine = lower == (lax.axis_index("fov") == 0)
    att_ref[...] = jnp.where(mine, knots / (1.0 + pltpu.roll(knots, 64, 1)), 0.0)


def calibration_kernel(in_ref, cal_ref, left_ref, right_ref):
    slots = in_ref[pl.ds(0, RANGES, stride=PIECES), :].T
    unit = slots[64:96].astype(jnp.int32)
    parts = wide_parts(slots[:64], 2)
    for k in range(CAP):
        lanes = slice(k * 128, (k + 1) * 128)
        inner = unit[k : k + 1]
        right_ref[:, lanes] = narrow_rows_equal(128, inner & 127)
        high = narrow_rows_equal(32, inner >> 7)
        for n in range(2):
            for v in range(2):
                row = jnp.broadcast_to(parts[n][v * 32 + k : v * 32 + k + 1], (32, 128)).astype(BF16)
                left_ref[(n * 2 + v) * 32 : (n * 2 + v + 1) * 32, lanes] = high * row
    sums = dot_nt(left_ref[...], right_ref[...])
    sums = sums[:64] + sums[64:]
    cal_ref[...] = sums[:32] / (1.0 + sums[32:])


VMEM = pl.BlockSpec(memory_space=pltpu.VMEM)
SMEM = pl.BlockSpec(memory_space=pltpu.SMEM)
LONG_ROW = pl.BlockSpec((1, 1, LONG), lambda s: (s, 0, 0))
WIDE_ROW = pl.BlockSpec((1, 1, WIDE), lambda s: (s, 0, 0))


def on_chip(*arrays):
    return [pltpu.with_memory_space_constraint(a, pltpu.VMEM) for a in arrays]


def off_chip(*arrays):
    return [pltpu.with_memory_space_constraint(a, pltpu.HBM) for a in arrays]


def whole(shape):
    return pl.BlockSpec(shape, lambda s: (0,) * len(shape))


def shards(
    src_partials,
    att_partials,
    cal_partials,
    obs_phase,
    obs_residual,
    block_source,
    block_segment,
    block_unit,
    live_blocks,
):
    source = block_source.reshape(WIDE_STEPS, 1, WIDE)
    segment = block_segment.reshape(WIDE_STEPS, 1, WIDE)
    unit = block_unit.reshape(WIDE_STEPS, 1, WIDE)
    src = jnp.transpose(src_partials, (1, 0, 2))
    att = att_partials.reshape(BLK * 4, OBS)
    sequential = pltpu.CompilerParams(dimension_semantics=("arbitrary",), vmem_limit_bytes=24 * 1024 * 1024)
    small = pltpu.CompilerParams(vmem_limit_bytes=4 * 1024 * 1024)
    keep, send, srct, src_low = pl.pallas_call(
        normals_kernel,
        grid=(WIDE_STEPS,),
        in_specs=[
            SMEM,
            pl.BlockSpec((5, WIDE, OBS), lambda s: (0, s, 0)),
            pl.BlockSpec((WIDE, OBS), lambda s: (s, 0)),
            WIDE_ROW,
        ],
        out_specs=[VMEM] * 4,
        out_shape=[
            pltpu.VMEM((20, 8, 256), F32),
            pltpu.VMEM((20, 8, 256), F32),
            pltpu.VMEM((6, OBS, BLK), F32),
            pltpu.VMEM((256, BLK), BF16),
        ],
        scratch_shapes=[pltpu.VMEM((320, 256), F32)],
        compiler_params=sequential,
        name="normals",
    )(live_blocks, *off_chip(src, obs_residual, source))
    half = pl.pallas_call(
        join_kernel,
        in_specs=[VMEM] * 2,
        out_specs=VMEM,
        out_shape=pltpu.VMEM((20, 8, 256), F32),
        compiler_params=small,
        name="join",
    )(*on_chip(keep, lax.ppermute(send, "fov", [(0, 1), (1, 0)])))
    half, live_later = lax.optimization_barrier((half, live_blocks))
    around = [lax.ppermute(half, "tm", [(i, i ^ d) for i in range(4)]) for d in (1, 2, 3)]
    extra, seg_low, owner, seg_high, place, diag_knots, diag_slots = pl.pallas_call(
        diag_kernel,
        grid=(WIDE_STEPS,),
        in_specs=[
            SMEM,
            pl.BlockSpec((WIDE * 4, OBS), lambda s: (s, 0)),
            pl.BlockSpec((WIDE, OBS), lambda s: (s, 0)),
            pl.BlockSpec((WIDE, OBS), lambda s: (s, 0)),
            WIDE_ROW,
            WIDE_ROW,
        ],
        out_specs=[VMEM] * 7,
        out_shape=[
            pltpu.VMEM((6, OBS, BLK), F32),
            pltpu.VMEM((128, BLK), BF16),
            pltpu.VMEM((RANGES, BLK), BF16),
            pltpu.VMEM((16, BLK), BF16),
            pltpu.VMEM((CAP, BLK), BF16),
            pltpu.VMEM((4, 16, 128), F32),
            pltpu.VMEM((64, RANGES), F32),
        ],
        scratch_shapes=[
            pltpu.VMEM((256, 128), F32),
            pltpu.VMEM((64, RANGES), F32),
            pltpu.VMEM((RANGES, CUT), F32),
        ],
        compiler_params=sequential,
        cost_estimate=pl.CostEstimate(flops=200_000_000, bytes_accessed=12_000_000, transcendentals=0),
        name="diag",
    )(live_later, att, obs_phase, cal_partials, segment, unit)
    around, diag_knots = lax.optimization_barrier((around, diag_knots))
    mine = pl.pallas_call(
        solve_kernel,
        in_specs=[VMEM] * 4,
        out_specs=VMEM,
        out_shape=pltpu.VMEM((5, 8, 256), F32),
        compiler_params=small,
        name="solve",
    )(*on_chip(half, *around))
    other = lax.ppermute(mine, "fov", [(0, 1), (1, 0)])
    outgoing, src_update = pl.pallas_call(
        apply_kernel,
        grid=(LONG_STEPS,),
        in_specs=[VMEM] * 7 + [LONG_ROW] + [VMEM] * 4,
        out_specs=[VMEM, whole((5, 4096))],
        out_shape=[
            pltpu.VMEM((128 * PIECES, 128), F32),
            jax.ShapeDtypeStruct((5, 4096), F32),
        ],
        scratch_shapes=[
            pltpu.VMEM((240, 256), BF16),
            pltpu.VMEM((256, 128), F32),
            pltpu.VMEM((CAP, RANGES), F32),
        ],
        compiler_params=sequential,
        name="apply",
    )(
        *on_chip(srct, extra, src_low, seg_low, owner, seg_high, place),
        source.reshape(LONG_STEPS, 1, LONG),
        *on_chip(mine, other, diag_knots, diag_slots),
    )
    arrived = lax.all_to_all(
        outgoing.reshape(128, 1, PIECES * 128), ALL, split_axis=0, concat_axis=0, tiled=True
    ).reshape(128 * PIECES, 128)
    att_half = pl.pallas_call(
        attitude_kernel,
        in_specs=[VMEM],
        out_specs=VMEM,
        out_shape=pltpu.VMEM((4, 128), F32),
        compiler_params=small,
        name="attitude",
    )(*on_chip(arrived))
    att_other = lax.ppermute(att_half, "fov", [(0, 1), (1, 0)])
    cal_update = pl.pallas_call(
        calibration_kernel,
        in_specs=[VMEM],
        out_specs=VMEM,
        out_shape=jax.ShapeDtypeStruct((32, 128), F32),
        scratch_shapes=[pltpu.VMEM((128, CAP * 128), BF16), pltpu.VMEM((128, CAP * 128), BF16)],
        cost_estimate=pl.CostEstimate(flops=100_000_000, bytes_accessed=400_000, transcendentals=0),
        name="calibration",
    )(*on_chip(arrived))
    att_update = att_half + att_other
    return (src_update, att_update.reshape(4, 1, 128), cal_update.reshape(SHARE))


def solution(mesh):
    return jax.shard_map(
        shards,
        mesh=mesh,
        in_specs=(
            P(ALL, None, None),
            P(ALL, None, None),
            P(ALL, None),
            P(ALL, None),
            P(ALL, None),
            P(ALL),
            P(ALL),
            P(ALL),
            P(ALL),
        ),
        out_specs=(P(None, "sky"), P(None, "tm", "sky"), P(ALL)),
        check_vma=False,
    )
```

```python
import jax
import jax.numpy as jnp
from jax import lax
from jax.experimental import pallas as pl
from jax.experimental.pallas import tpu as pltpu
from jax.sharding import PartitionSpec as P

BLK = 2048
CUT = 256
WIDE = 512
WIDE_STEPS = BLK // WIDE
LONG = 2048
LONG_STEPS = BLK // LONG
OBS = 128
CAP = 32
RANGES = 128
SHARE = 4096
PIECES = 5
F32 = jnp.float32
BF16 = jnp.bfloat16
ALL = ("sky", "tm", "fov")

index_pairs = [(i, j) for i in range(5) for j in range(i, 5)]


def split_parts(x, count):
    parts = []
    for _ in range(count - 1):
        part = x.astype(BF16)
        parts.append(part)
        x = x - part.astype(F32)
    parts.append(x.astype(BF16))
    return parts


def dot_nt(a, b):
    return lax.dot_general(a, b, (((1,), (1,)), ((), ())), preferred_element_type=F32)


def dot_nn(a, b):
    return lax.dot_general(a, b, (((1,), (0,)), ((), ())), preferred_element_type=F32)


def rows_equal(count, row):
    iota = lax.broadcasted_iota(jnp.int32, (count, row.shape[1]), 0)
    return jnp.where(iota == row, 1.0, 0.0)


def narrow_rows_equal(count, row):
    iota = lax.broadcasted_iota(jnp.int32, (count, row.shape[1]), 0).astype(F32).astype(BF16)
    wide = jnp.broadcast_to(row.astype(F32), (count, row.shape[1])).astype(BF16)
    return jnp.where(iota == wide, jnp.ones((), BF16), jnp.zeros((), BF16))


def accumulate(ref, product, step):
    @pl.when(step == 0)
    def _():
        ref[...] = product

    @pl.when(step > 0)
    def _():
        ref[...] += product


def live_row(live_ref, step, width):
    position = step * width + lax.broadcasted_iota(jnp.int32, (1, width), 1)
    return jnp.where(position < live_ref[0], 1.0, 0.0)


def columns(step, width):
    return pl.ds(pl.multiple_of(step * width, width), width)


def row_bit(bit):
    return (lax.broadcasted_iota(jnp.int32, (8, 128), 0) & bit) == 0


def fold(accs):
    upper = row_bit(4)
    level = [
        jnp.where(upper, accs[i], accs[i + 4]) + pltpu.roll(jnp.where(upper, accs[i + 4], accs[i]), 4, 0)
        for i in range(4)
    ]
    upper = row_bit(2)
    level = [
        jnp.where(upper, level[i], level[i + 2])
        + jnp.where(upper, pltpu.roll(level[i], 6, 0), pltpu.roll(level[i + 2], 2, 0))
        for i in range(2)
    ]
    upper = row_bit(1)
    return jnp.where(upper, level[0], level[1]) + jnp.where(
        upper, pltpu.roll(level[0], 7, 0), pltpu.roll(level[1], 1, 0)
    )


def wide_parts(x, count):
    parts = []
    for _ in range(count - 1):
        part = x.astype(BF16).astype(F32)
        parts.append(part)
        x = x - part
    return parts + [x]


def masked_rows(mask, blocks, count):
    sides = []
    split = [wide_parts(block, count) for block in blocks]
    for n in range(count):
        pieces = []
        for parts in split:
            for k in range(parts[n].shape[0]):
                pieces.append(mask * jnp.broadcast_to(parts[n][k : k + 1], mask.shape).astype(BF16))
        sides.append(jnp.concatenate(pieces, axis=0))
    return jnp.concatenate(sides, axis=1)


def repeated_dot(left, right, count):
    return dot_nt(left, jnp.concatenate([right] * count, axis=1))


def column_sum(x):
    return jnp.sum(x, axis=0, keepdims=True)


def spline_basis(phase):
    rest = 1.0 - phase
    square = phase * phase
    cubed = square * phase
    half = 0.5 * cubed
    return (
        rest * rest * rest * (1.0 / 6.0),
        half - square + (2.0 / 3.0),
        0.5 * (square + phase) - half + (1.0 / 6.0),
        cubed * (1.0 / 6.0),
    )


def spline_from_moments(m, j):
    sixth = 1.0 / 6.0
    if j == 0:
        return (m[0] - m[3]) * sixth + 0.5 * (m[2] - m[1])
    if j == 1:
        return m[0] * (2.0 / 3.0) - m[2] + 0.5 * m[3]
    if j == 2:
        return m[0] * sixth + 0.5 * (m[1] + m[2] - m[3])
    return m[3] * sixth


def normals_kernel(live_ref, src_ref, res_ref, idx_ref, keep_ref, send_ref, all_src_ref, all_low_ref, acc_ref, left_ref):
    step = pl.program_id(0)
    span = columns(step, WIDE)
    srct_ref = all_src_ref.at[:, :, span]
    idx = idx_ref[0] ^ (lax.axis_index("fov") * 2048)
    live = live_row(live_ref, step, WIDE)
    earlier = columns(jnp.maximum(step - 1, 0), WIDE)
    product = repeated_dot(left_ref[...], all_low_ref[:, earlier], 3)
    acc_ref[...] = jnp.where(step > 1, acc_ref[...], 0.0) + jnp.where(step > 0, product, 0.0)
    sides = []
    for part in range(WIDE // CUT):
        cut = slice(part * CUT, (part + 1) * CUT)
        high = (rows_equal(16, idx[:, cut] >> 8) * live[:, cut]).astype(BF16)
        low = narrow_rows_equal(256, idx[:, cut] & 255)
        all_low_ref[:, columns(step * (WIDE // CUT) + part, CUT)] = low
        groups = []
        spare = []
        for h in range(CUT // 128):
            lanes = slice(part * CUT + h * 128, part * CUT + (h + 1) * 128)
            for i in range(5):
                srct_ref[i, :, lanes] = src_ref[i, lanes, :].T
            srct_ref[5, :, lanes] = res_ref[lanes, :].T
            sums = [None] * 20
            for o in range(OBS // 8):
                rows = [srct_ref[i, o * 8 : o * 8 + 8, lanes] for i in range(6)]
                terms = [rows[i] * rows[j] for i, j in index_pairs] + [rows[i] * rows[5] for i in range(5)]
                sums = terms if o == 0 else [s + t for s, t in zip(sums, terms)]
            groups.append(jnp.concatenate([fold(sums[:8]), fold(sums[8:16])], axis=0))
            spare.append(sums[16:])
        both = fold(spare[0] + spare[1])
        blocks = [jnp.concatenate(groups, axis=1), jnp.concatenate([both[:4], both[4:]], axis=1)]
        sides.append(masked_rows(high, blocks, 3))
    left_ref[...] = jnp.concatenate(
        [side[:, n * CUT : (n + 1) * CUT] for n in range(3) for side in sides], axis=1
    )

    @pl.when(step == WIDE_STEPS - 1)
    def _():
        last = repeated_dot(left_ref[...], all_low_ref[:, columns(step, WIDE)], 3)
        for k in range(20):
            row = k * 16
            keep_ref[k] = acc_ref[row : row + 8] + last[row : row + 8]
            send_ref[k] = acc_ref[row + 8 : row + 16] + last[row + 8 : row + 16]


def shifted(rows, distance):
    moved = pltpu.roll(rows, distance, 1)
    below = pltpu.roll(moved, 1, 0)
    row = lax.broadcasted_iota(jnp.int32, rows.shape, 0)
    lane = lax.broadcasted_iota(jnp.int32, rows.shape, 1)
    return jnp.where(lane >= distance, moved, jnp.where(row > 0, below, 0.0))


def knots_of(parts):
    total = parts[0]
    for j in range(1, 4):
        total = total + shifted(parts[j], j)
    return total


def diag_kernel(
    live_ref, att_ref, pha_ref, cal_ref, seg_ref, unit_ref,
    all_extra_ref, all_low_ref, all_owner_ref, all_high_ref, all_place_ref, knots_ref, slots_ref,
    acc_ref, slot_ref, carry_ref,
):
    step = pl.program_id(0)
    span = columns(step, WIDE)
    extra_ref = all_extra_ref.at[:, :, span]
    live = live_row(live_ref, step, WIDE)
    unit = unit_ref[0]
    owner = rows_equal(RANGES, unit >> 12)
    owner_low = owner.astype(BF16)
    all_owner_ref[:, span] = owner_low
    before = lax.broadcasted_iota(jnp.int32, (CUT, CUT), 0) < lax.broadcasted_iota(jnp.int32, (CUT, CUT), 1)
    before = jnp.where(before, 1.0, 0.0).astype(BF16)
    carry = jnp.where(step > 0, carry_ref[...], 0.0)
    ranks = []
    for h in range(WIDE // CUT):
        part = slice(h * CUT, (h + 1) * CUT)
        earlier = dot_nn(owner_low[:, part], before) + carry
        ranks.append(column_sum(owner[:, part] * earlier))
        carry = carry + dot_nn(owner_low[:, part], jnp.ones((CUT, CUT), BF16))
    carry_ref[...] = carry
    rank = jnp.concatenate(ranks, axis=1).astype(jnp.int32)
    place = rows_equal(CAP, rank)
    place_live = (place * live).astype(BF16)
    all_place_ref[:, span] = place_live
    seg = seg_ref[0]
    seg_high = (rows_equal(16, seg >> 7) * live).astype(BF16)
    seg_low = narrow_rows_equal(128, seg & 127)
    all_high_ref[:, span] = seg_high
    all_low_ref[:, span] = seg_low
    groups = []
    units = []
    for h in range(WIDE // 128):
        lanes = slice(h * 128, (h + 1) * 128)
        for c in range(4):
            extra_ref[c, :, lanes] = att_ref[pl.ds(h * 512 + c, 128, stride=4), :].T
        extra_ref[4, :, lanes] = pha_ref[lanes, :].T
        extra_ref[5, :, lanes] = cal_ref[lanes, :].T
        sums = [None] * 17
        for o in range(OBS // 8):
            rows = [extra_ref[i, o * 8 : o * 8 + 8, lanes] for i in range(6)]
            basis = [b * b for b in spline_basis(rows[4])]
            squares = [rows[c] * rows[c] for c in range(4)]
            terms = [b * s for b in basis for s in squares] + [rows[5] * rows[5]]
            sums = terms if o == 0 else [s + t for s, t in zip(sums, terms)]
        groups.append(jnp.concatenate([fold(sums[:8]), fold(sums[8:16])], axis=0))
        units.append(column_sum(sums[16]))
    left = masked_rows(seg_high, [jnp.concatenate(groups, axis=1)], 2)
    accumulate(acc_ref, repeated_dot(left, seg_low, 2), step)
    inner = (unit & (SHARE - 1)).astype(F32)
    left = jnp.concatenate(
        [
            masked_rows(place_live, [jnp.concatenate(units, axis=1)], 2),
            masked_rows(place.astype(BF16), [inner], 2),
        ],
        axis=0,
    )
    accumulate(slot_ref, repeated_dot(left, owner_low, 2), step)

    @pl.when(step == WIDE_STEPS - 1)
    def _():
        for c in range(4):
            knots_ref[c] = knots_of([acc_ref[(j * 4 + c) * 16 : (j * 4 + c) * 16 + 16] for j in range(4)])
        slots_ref[...] = slot_ref[...]


def join_kernel(a_ref, b_ref, out_ref):
    out_ref[...] = a_ref[...] + b_ref[...]


def solve_kernel(a_ref, b_ref, c_ref, d_ref, out_ref):
    packed = [(a_ref[k] + c_ref[k]) + (b_ref[k] + d_ref[k]) for k in range(20)]
    matrix = {}
    for position, (i, j) in enumerate(index_pairs):
        matrix[i, j] = packed[position] + (1.0 if i == j else 0.0)
    factor = {}
    inverse = {}
    for i in range(5):
        for j in range(i + 1):
            running = matrix[j, i]
            for k in range(j):
                running = running - factor[i, k] * factor[j, k]
            if i == j:
                inverse[i] = 1.0 / jnp.sqrt(running)
            else:
                factor[i, j] = running * inverse[j]
    forward = []
    for i in range(5):
        running = packed[15 + i]
        for k in range(i):
            running = running - factor[i, k] * forward[k]
        forward.append(running * inverse[i])
    result = [None] * 5
    for i in reversed(range(5)):
        running = forward[i]
        for k in range(i + 1, 5):
            running = running - factor[k, i] * result[k]
        result[i] = running * inverse[i]
        out_ref[i] = result[i]


def apply_kernel(
    all_src_ref, all_extra_ref, src_low_ref, seg_low_ref, owner_ref, seg_high_ref, place_ref, idx_ref,
    mine_ref, other_ref, diag_ref, slots_ref, out_ref, update_ref, table_ref, acc_ref, slot_ref,
):
    step = pl.program_id(0)
    span = columns(step, LONG)
    srct_ref = all_src_ref.at[:, :, span]
    extra_ref = all_extra_ref.at[:, :, span]
    fov = lax.axis_index("fov")

    @pl.when(step == 0)
    def _():
        out_ref[...] = jnp.zeros_like(out_ref)
        pieces = []
        for k in range(5):
            mine = mine_ref[k]
            other = other_ref[k]
            pieces += [mine, other]
            first = jnp.where(fov == 0, mine, other)
            second = jnp.where(fov == 0, other, mine)
            for q in range(8):
                update_ref[k : k + 1, q * 256 : (q + 1) * 256] = first[q : q + 1]
                update_ref[k : k + 1, 2048 + q * 256 : 2048 + (q + 1) * 256] = second[q : q + 1]
        stacked = jnp.concatenate(pieces, axis=0)
        table_ref[...] = jnp.concatenate(split_parts(stacked, 3), axis=0)

    idx = idx_ref[0] ^ (fov * 2048)
    knot_sums = None
    slot_sums = None
    for part in range(LONG // CUT):
        cut = slice(part * CUT, (part + 1) * CUT)
        place = columns(step * (LONG // CUT) + part, CUT)
        high = rows_equal(16, idx[:, cut] >> 8)
        looked = dot_nn(table_ref[...], src_low_ref[:, place])
        looked = looked[:80] + looked[80:160] + looked[160:]
        chosen = [column_sum(looked[k * 16 : k * 16 + 16] * high) for k in range(5)]
        groups = []
        units = []
        for h in range(CUT // 128):
            lanes = slice(part * CUT + h * 128, part * CUT + (h + 1) * 128)
            spread = [jnp.broadcast_to(chosen[k][:, h * 128 : (h + 1) * 128], (8, 128)) for k in range(5)]
            sums = [None] * 17
            for o in range(OBS // 8):
                rows = slice(o * 8, o * 8 + 8)
                model = srct_ref[0, rows, lanes] * spread[0]
                for k in range(1, 5):
                    model = model + srct_ref[k, rows, lanes] * spread[k]
                residual = srct_ref[5, rows, lanes] - model
                phase = extra_ref[4, rows, lanes]
                moments = [extra_ref[c, rows, lanes] * residual for c in range(4)]
                terms = list(moments)
                for _ in range(3):
                    moments = [m * phase for m in moments]
                    terms += moments
                terms.append(extra_ref[5, rows, lanes] * residual)
                sums = terms if o == 0 else [s + t for s, t in zip(sums, terms)]
            groups.append(jnp.concatenate([fold(sums[:8]), fold(sums[8:16])], axis=0))
            units.append(column_sum(sums[16]))
        left = masked_rows(seg_high_ref[:, place], [jnp.concatenate(groups, axis=1)], 2)
        knot_part = repeated_dot(left, seg_low_ref[:, place], 2)
        left = masked_rows(place_ref[:, place], [jnp.concatenate(units, axis=1)], 2)
        slot_part = repeated_dot(left, owner_ref[:, place], 2)
        knot_sums = knot_part if part == 0 else knot_sums + knot_part
        slot_sums = slot_part if part == 0 else slot_sums + slot_part
    accumulate(acc_ref, knot_sums, step)
    accumulate(slot_ref, slot_sums, step)

    @pl.when(step == LONG_STEPS - 1)
    def _():
        tm = lax.axis_index("tm")
        slots = jnp.concatenate([slot_ref[...], slots_ref[...], jnp.zeros((CAP, RANGES), F32)], axis=0)
        out_ref[pl.ds(0, RANGES, stride=PIECES), :] = slots.T
        first_half = lax.broadcasted_iota(jnp.int32, (16, 128), 1) < 64
        for c in range(4):
            moments = [acc_ref[(k * 4 + c) * 16 : (k * 4 + c) * 16 + 16] for k in range(4)]
            right = knots_of([spline_from_moments(moments, j) for j in range(4)])
            far = pltpu.roll(diag_ref[c], 64, 1)
            start = tm * 2 * PIECES + 1 + c
            out_ref[pl.ds(start, 16, stride=8 * PIECES), :] = jnp.where(first_half, right, far)
            out_ref[pl.ds(start + PIECES, 16, stride=8 * PIECES), :] = jnp.where(first_half, far, right)


def attitude_kernel(in_ref, att_ref):
    base = lax.axis_index("tm") * 2 * PIECES + 1
    knots = None
    for s in range(16):
        for f in range(2):
            part = in_ref[pl.ds(base + (s * 8 + f) * PIECES, 4), :]
            knots = part if knots is None else knots + part
    lower = lax.broadcasted_iota(jnp.int32, (4, 128), 1) < 64
    mine = lower == (lax.axis_index("fov") == 0)
    att_ref[...] = jnp.where(mine, knots / (1.0 + pltpu.roll(knots, 64, 1)), 0.0)


def calibration_kernel(in_ref, cal_ref, left_ref, right_ref):
    slots = in_ref[pl.ds(0, RANGES, stride=PIECES), :].T
    unit = slots[64:96].astype(jnp.int32)
    parts = wide_parts(slots[:64], 2)
    for k in range(CAP):
        lanes = slice(k * 128, (k + 1) * 128)
        inner = unit[k : k + 1]
        right_ref[:, lanes] = narrow_rows_equal(128, inner & 127)
        high = narrow_rows_equal(32, inner >> 7)
        for n in range(2):
            for v in range(2):
                row = jnp.broadcast_to(parts[n][v * 32 + k : v * 32 + k + 1], (32, 128)).astype(BF16)
                left_ref[(n * 2 + v) * 32 : (n * 2 + v + 1) * 32, lanes] = high * row
    sums = dot_nt(left_ref[...], right_ref[...])
    sums = sums[:64] + sums[64:]
    cal_ref[...] = sums[:32] / (1.0 + sums[32:])


VMEM = pl.BlockSpec(memory_space=pltpu.VMEM)
SMEM = pl.BlockSpec(memory_space=pltpu.SMEM)
LONG_ROW = pl.BlockSpec((1, 1, LONG), lambda s: (s, 0, 0))
WIDE_ROW = pl.BlockSpec((1, 1, WIDE), lambda s: (s, 0, 0))


def on_chip(*arrays):
    return [pltpu.with_memory_space_constraint(a, pltpu.VMEM) for a in arrays]


def off_chip(*arrays):
    return [pltpu.with_memory_space_constraint(a, pltpu.HBM) for a in arrays]


def whole(shape):
    return pl.BlockSpec(shape, lambda s: (0,) * len(shape))


def shards(
    src_partials,
    att_partials,
    cal_partials,
    obs_phase,
    obs_residual,
    block_source,
    block_segment,
    block_unit,
    live_blocks,
):
    source = block_source.reshape(WIDE_STEPS, 1, WIDE)
    segment = block_segment.reshape(WIDE_STEPS, 1, WIDE)
    unit = block_unit.reshape(WIDE_STEPS, 1, WIDE)
    src = jnp.transpose(src_partials, (1, 0, 2))
    att = att_partials.reshape(BLK * 4, OBS)
    sequential = pltpu.CompilerParams(dimension_semantics=("arbitrary",), vmem_limit_bytes=24 * 1024 * 1024)
    small = pltpu.CompilerParams(vmem_limit_bytes=4 * 1024 * 1024)
    keep, send, srct, src_low = pl.pallas_call(
        normals_kernel,
        grid=(WIDE_STEPS,),
        in_specs=[
            SMEM,
            pl.BlockSpec((5, WIDE, OBS), lambda s: (0, s, 0)),
            pl.BlockSpec((WIDE, OBS), lambda s: (s, 0)),
            WIDE_ROW,
        ],
        out_specs=[VMEM] * 4,
        out_shape=[
            pltpu.VMEM((20, 8, 256), F32),
            pltpu.VMEM((20, 8, 256), F32),
            pltpu.VMEM((6, OBS, BLK), F32),
            pltpu.VMEM((256, BLK), BF16),
        ],
        scratch_shapes=[pltpu.VMEM((320, 256), F32), pltpu.VMEM((320, 3 * WIDE), BF16)],
        compiler_params=sequential,
        name="normals",
    )(live_blocks, *off_chip(src, obs_residual, source))
    half = pl.pallas_call(
        join_kernel,
        in_specs=[VMEM] * 2,
        out_specs=VMEM,
        out_shape=pltpu.VMEM((20, 8, 256), F32),
        compiler_params=small,
        name="join",
    )(*on_chip(keep, lax.ppermute(send, "fov", [(0, 1), (1, 0)])))
    half, live_later = lax.optimization_barrier((half, live_blocks))
    around = [lax.ppermute(half, "tm", [(i, i ^ d) for i in range(4)]) for d in (1, 2, 3)]
    extra, seg_low, owner, seg_high, place, diag_knots, diag_slots = pl.pallas_call(
        diag_kernel,
        grid=(WIDE_STEPS,),
        in_specs=[
            SMEM,
            pl.BlockSpec((WIDE * 4, OBS), lambda s: (s, 0)),
            pl.BlockSpec((WIDE, OBS), lambda s: (s, 0)),
            pl.BlockSpec((WIDE, OBS), lambda s: (s, 0)),
            WIDE_ROW,
            WIDE_ROW,
        ],
        out_specs=[VMEM] * 7,
        out_shape=[
            pltpu.VMEM((6, OBS, BLK), F32),
            pltpu.VMEM((128, BLK), BF16),
            pltpu.VMEM((RANGES, BLK), BF16),
            pltpu.VMEM((16, BLK), BF16),
            pltpu.VMEM((CAP, BLK), BF16),
            pltpu.VMEM((4, 16, 128), F32),
            pltpu.VMEM((64, RANGES), F32),
        ],
        scratch_shapes=[
            pltpu.VMEM((256, 128), F32),
            pltpu.VMEM((64, RANGES), F32),
            pltpu.VMEM((RANGES, CUT), F32),
        ],
        compiler_params=sequential,
        cost_estimate=pl.CostEstimate(flops=200_000_000, bytes_accessed=12_000_000, transcendentals=0),
        name="diag",
    )(live_later, att, obs_phase, cal_partials, segment, unit)
    around, diag_knots = lax.optimization_barrier((around, diag_knots))
    mine = pl.pallas_call(
        solve_kernel,
        in_specs=[VMEM] * 4,
        out_specs=VMEM,
        out_shape=pltpu.VMEM((5, 8, 256), F32),
        compiler_params=small,
        name="solve",
    )(*on_chip(half, *around))
    other = lax.ppermute(mine, "fov", [(0, 1), (1, 0)])
    outgoing, src_update = pl.pallas_call(
        apply_kernel,
        grid=(LONG_STEPS,),
        in_specs=[VMEM] * 7 + [LONG_ROW] + [VMEM] * 4,
        out_specs=[VMEM, whole((5, 4096))],
        out_shape=[
            pltpu.VMEM((128 * PIECES, 128), F32),
            jax.ShapeDtypeStruct((5, 4096), F32),
        ],
        scratch_shapes=[
            pltpu.VMEM((240, 256), BF16),
            pltpu.VMEM((256, 128), F32),
            pltpu.VMEM((CAP, RANGES), F32),
        ],
        compiler_params=sequential,
        name="apply",
    )(
        *on_chip(srct, extra, src_low, seg_low, owner, seg_high, place),
        source.reshape(LONG_STEPS, 1, LONG),
        *on_chip(mine, other, diag_knots, diag_slots),
    )
    arrived = lax.all_to_all(
        outgoing.reshape(128, 1, PIECES * 128), ALL, split_axis=0, concat_axis=0, tiled=True
    ).reshape(128 * PIECES, 128)
    att_half = pl.pallas_call(
        attitude_kernel,
        in_specs=[VMEM],
        out_specs=VMEM,
        out_shape=pltpu.VMEM((4, 128), F32),
        compiler_params=small,
        name="attitude",
    )(*on_chip(arrived))
    att_other = lax.ppermute(att_half, "fov", [(0, 1), (1, 0)])
    cal_update = pl.pallas_call(
        calibration_kernel,
        in_specs=[VMEM],
        out_specs=VMEM,
        out_shape=jax.ShapeDtypeStruct((32, 128), F32),
        scratch_shapes=[pltpu.VMEM((128, CAP * 128), BF16), pltpu.VMEM((128, CAP * 128), BF16)],
        cost_estimate=pl.CostEstimate(flops=100_000_000, bytes_accessed=400_000, transcendentals=0),
        name="calibration",
    )(*on_chip(arrived))
    att_update = att_half + att_other
    return (src_update, att_update.reshape(4, 1, 128), cal_update.reshape(SHARE))


def solution(mesh):
    return jax.shard_map(
        shards,
        mesh=mesh,
        in_specs=(
            P(ALL, None, None),
            P(ALL, None, None),
            P(ALL, None),
            P(ALL, None),
            P(ALL, None),
            P(ALL),
            P(ALL),
            P(ALL),
            P(ALL),
        ),
        out_specs=(P(None, "sky"), P(None, "tm", "sky"), P(ALL)),
        check_vma=False,
    )
```

```python
import jax
import jax.numpy as jnp
from jax import lax
from jax.experimental import pallas as pl
from jax.experimental.pallas import tpu as pltpu
from jax.sharding import PartitionSpec as P

BLK = 2048
CUT = 256
WIDE = 1024
WIDE_STEPS = BLK // WIDE
LONG = 2048
LONG_STEPS = BLK // LONG
OBS = 128
CAP = 32
RANGES = 128
SHARE = 4096
PIECES = 5
F32 = jnp.float32
BF16 = jnp.bfloat16
ALL = ("sky", "tm", "fov")

index_pairs = [(i, j) for i in range(5) for j in range(i, 5)]


def split_parts(x, count):
    parts = []
    for _ in range(count - 1):
        part = x.astype(BF16)
        parts.append(part)
        x = x - part.astype(F32)
    parts.append(x.astype(BF16))
    return parts


def dot_nt(a, b):
    return lax.dot_general(a, b, (((1,), (1,)), ((), ())), preferred_element_type=F32)


def dot_nn(a, b):
    return lax.dot_general(a, b, (((1,), (0,)), ((), ())), preferred_element_type=F32)


def rows_equal(count, row):
    iota = lax.broadcasted_iota(jnp.int32, (count, row.shape[1]), 0)
    return jnp.where(iota == row, 1.0, 0.0)


def narrow_rows_equal(count, row):
    iota = lax.broadcasted_iota(jnp.int32, (count, row.shape[1]), 0).astype(F32).astype(BF16)
    wide = jnp.broadcast_to(row.astype(F32), (count, row.shape[1])).astype(BF16)
    return jnp.where(iota == wide, jnp.ones((), BF16), jnp.zeros((), BF16))


def accumulate(ref, product, step):
    @pl.when(step == 0)
    def _():
        ref[...] = product

    @pl.when(step > 0)
    def _():
        ref[...] += product


def live_row(live_ref, step, width):
    position = step * width + lax.broadcasted_iota(jnp.int32, (1, width), 1)
    return jnp.where(position < live_ref[0], 1.0, 0.0)


def columns(step, width):
    return pl.ds(pl.multiple_of(step * width, width), width)


def row_bit(bit):
    return (lax.broadcasted_iota(jnp.int32, (8, 128), 0) & bit) == 0


def fold(accs):
    upper = row_bit(4)
    level = [
        jnp.where(upper, accs[i], accs[i + 4]) + pltpu.roll(jnp.where(upper, accs[i + 4], accs[i]), 4, 0)
        for i in range(4)
    ]
    upper = row_bit(2)
    level = [
        jnp.where(upper, level[i], level[i + 2])
        + jnp.where(upper, pltpu.roll(level[i], 6, 0), pltpu.roll(level[i + 2], 2, 0))
        for i in range(2)
    ]
    upper = row_bit(1)
    return jnp.where(upper, level[0], level[1]) + jnp.where(
        upper, pltpu.roll(level[0], 7, 0), pltpu.roll(level[1], 1, 0)
    )


def wide_parts(x, count):
    parts = []
    for _ in range(count - 1):
        part = x.astype(BF16).astype(F32)
        parts.append(part)
        x = x - part
    return parts + [x]


def masked_rows(mask, blocks, count):
    sides = []
    split = [wide_parts(block, count) for block in blocks]
    for n in range(count):
        pieces = []
        for parts in split:
            for k in range(parts[n].shape[0]):
                pieces.append(mask * jnp.broadcast_to(parts[n][k : k + 1], mask.shape).astype(BF16))
        sides.append(jnp.concatenate(pieces, axis=0))
    return jnp.concatenate(sides, axis=1)


def repeated_dot(left, right, count):
    return dot_nt(left, jnp.concatenate([right] * count, axis=1))


def column_sum(x):
    return jnp.sum(x, axis=0, keepdims=True)


def spline_basis(phase):
    rest = 1.0 - phase
    square = phase * phase
    cubed = square * phase
    half = 0.5 * cubed
    return (
        rest * rest * rest * (1.0 / 6.0),
        half - square + (2.0 / 3.0),
        0.5 * (square + phase) - half + (1.0 / 6.0),
        cubed * (1.0 / 6.0),
    )


def spline_from_moments(m, j):
    sixth = 1.0 / 6.0
    if j == 0:
        return (m[0] - m[3]) * sixth + 0.5 * (m[2] - m[1])
    if j == 1:
        return m[0] * (2.0 / 3.0) - m[2] + 0.5 * m[3]
    if j == 2:
        return m[0] * sixth + 0.5 * (m[1] + m[2] - m[3])
    return m[3] * sixth


def normals_kernel(live_ref, src_ref, res_ref, idx_ref, keep_ref, send_ref, all_src_ref, all_low_ref, acc_ref):
    step = pl.program_id(0)
    span = columns(step, WIDE)
    srct_ref = all_src_ref.at[:, :, span]
    idx = idx_ref[0] ^ (lax.axis_index("fov") * 2048)
    live = live_row(live_ref, step, WIDE)
    total = None
    for part in range(WIDE // CUT):
        cut = slice(part * CUT, (part + 1) * CUT)
        high = (rows_equal(16, idx[:, cut] >> 8) * live[:, cut]).astype(BF16)
        low = narrow_rows_equal(256, idx[:, cut] & 255)
        all_low_ref[:, columns(step * (WIDE // CUT) + part, CUT)] = low
        groups = []
        spare = []
        for h in range(CUT // 128):
            lanes = slice(part * CUT + h * 128, part * CUT + (h + 1) * 128)
            for i in range(5):
                srct_ref[i, :, lanes] = src_ref[i, lanes, :].T
            srct_ref[5, :, lanes] = res_ref[lanes, :].T
            sums = [None] * 20
            for o in range(OBS // 8):
                rows = [srct_ref[i, o * 8 : o * 8 + 8, lanes] for i in range(6)]
                terms = [rows[i] * rows[j] for i, j in index_pairs] + [rows[i] * rows[5] for i in range(5)]
                sums = terms if o == 0 else [s + t for s, t in zip(sums, terms)]
            groups.append(jnp.concatenate([fold(sums[:8]), fold(sums[8:16])], axis=0))
            spare.append(sums[16:])
        both = fold(spare[0] + spare[1])
        blocks = [jnp.concatenate(groups, axis=1), jnp.concatenate([both[:4], both[4:]], axis=1)]
        product = repeated_dot(masked_rows(high, blocks, 3), low, 3)
        total = product if part == 0 else total + product
    accumulate(acc_ref, total, step)

    @pl.when(step == WIDE_STEPS - 1)
    def _():
        for k in range(20):
            keep_ref[k] = acc_ref[k * 16 : k * 16 + 8]
            send_ref[k] = acc_ref[k * 16 + 8 : k * 16 + 16]


def shifted(rows, distance):
    moved = pltpu.roll(rows, distance, 1)
    below = pltpu.roll(moved, 1, 0)
    row = lax.broadcasted_iota(jnp.int32, rows.shape, 0)
    lane = lax.broadcasted_iota(jnp.int32, rows.shape, 1)
    return jnp.where(lane >= distance, moved, jnp.where(row > 0, below, 0.0))


def knots_of(parts):
    total = parts[0]
    for j in range(1, 4):
        total = total + shifted(parts[j], j)
    return total


def diag_kernel(
    live_ref, att_ref, pha_ref, cal_ref, seg_ref, unit_ref,
    all_extra_ref, all_low_ref, all_owner_ref, all_high_ref, all_place_ref, knots_ref, slots_ref,
    acc_ref, slot_ref, carry_ref,
):
    step = pl.program_id(0)
    span = columns(step, WIDE)
    extra_ref = all_extra_ref.at[:, :, span]
    live = live_row(live_ref, step, WIDE)
    unit = unit_ref[0]
    owner = rows_equal(RANGES, unit >> 12)
    owner_low = owner.astype(BF16)
    all_owner_ref[:, span] = owner_low
    before = lax.broadcasted_iota(jnp.int32, (CUT, CUT), 0) < lax.broadcasted_iota(jnp.int32, (CUT, CUT), 1)
    before = jnp.where(before, 1.0, 0.0).astype(BF16)
    carry = jnp.where(step > 0, carry_ref[...], 0.0)
    ranks = []
    for h in range(WIDE // CUT):
        part = slice(h * CUT, (h + 1) * CUT)
        earlier = dot_nn(owner_low[:, part], before) + carry
        ranks.append(column_sum(owner[:, part] * earlier))
        carry = carry + dot_nn(owner_low[:, part], jnp.ones((CUT, CUT), BF16))
    carry_ref[...] = carry
    rank = jnp.concatenate(ranks, axis=1).astype(jnp.int32)
    place = rows_equal(CAP, rank)
    place_live = (place * live).astype(BF16)
    all_place_ref[:, span] = place_live
    seg = seg_ref[0]
    seg_high = (rows_equal(16, seg >> 7) * live).astype(BF16)
    seg_low = narrow_rows_equal(128, seg & 127)
    all_high_ref[:, span] = seg_high
    all_low_ref[:, span] = seg_low
    groups = []
    units = []
    for h in range(WIDE // 128):
        lanes = slice(h * 128, (h + 1) * 128)
        for c in range(4):
            extra_ref[c, :, lanes] = att_ref[pl.ds(h * 512 + c, 128, stride=4), :].T
        extra_ref[4, :, lanes] = pha_ref[lanes, :].T
        extra_ref[5, :, lanes] = cal_ref[lanes, :].T
        sums = [None] * 17
        for o in range(OBS // 8):
            rows = [extra_ref[i, o * 8 : o * 8 + 8, lanes] for i in range(6)]
            basis = [b * b for b in spline_basis(rows[4])]
            squares = [rows[c] * rows[c] for c in range(4)]
            terms = [b * s for b in basis for s in squares] + [rows[5] * rows[5]]
            sums = terms if o == 0 else [s + t for s, t in zip(sums, terms)]
        groups.append(jnp.concatenate([fold(sums[:8]), fold(sums[8:16])], axis=0))
        units.append(column_sum(sums[16]))
    left = masked_rows(seg_high, [jnp.concatenate(groups, axis=1)], 2)
    accumulate(acc_ref, repeated_dot(left, seg_low, 2), step)
    inner = (unit & (SHARE - 1)).astype(F32)
    left = jnp.concatenate(
        [
            masked_rows(place_live, [jnp.concatenate(units, axis=1)], 2),
            masked_rows(place.astype(BF16), [inner], 2),
        ],
        axis=0,
    )
    accumulate(slot_ref, repeated_dot(left, owner_low, 2), step)

    @pl.when(step == WIDE_STEPS - 1)
    def _():
        for c in range(4):
            knots_ref[c] = knots_of([acc_ref[(j * 4 + c) * 16 : (j * 4 + c) * 16 + 16] for j in range(4)])
        slots_ref[...] = slot_ref[...]


def join_kernel(a_ref, b_ref, out_ref):
    out_ref[...] = a_ref[...] + b_ref[...]


def solve_kernel(a_ref, b_ref, c_ref, d_ref, out_ref):
    packed = [(a_ref[k] + c_ref[k]) + (b_ref[k] + d_ref[k]) for k in range(20)]
    matrix = {}
    for position, (i, j) in enumerate(index_pairs):
        matrix[i, j] = packed[position] + (1.0 if i == j else 0.0)
    factor = {}
    inverse = {}
    for i in range(5):
        for j in range(i + 1):
            running = matrix[j, i]
            for k in range(j):
                running = running - factor[i, k] * factor[j, k]
            if i == j:
                inverse[i] = 1.0 / jnp.sqrt(running)
            else:
                factor[i, j] = running * inverse[j]
    forward = []
    for i in range(5):
        running = packed[15 + i]
        for k in range(i):
            running = running - factor[i, k] * forward[k]
        forward.append(running * inverse[i])
    result = [None] * 5
    for i in reversed(range(5)):
        running = forward[i]
        for k in range(i + 1, 5):
            running = running - factor[k, i] * result[k]
        result[i] = running * inverse[i]
        out_ref[i] = result[i]


def apply_kernel(
    all_src_ref, all_extra_ref, src_low_ref, seg_low_ref, owner_ref, seg_high_ref, place_ref, idx_ref,
    mine_ref, other_ref, diag_ref, slots_ref, out_ref, update_ref, table_ref, acc_ref, slot_ref,
):
    step = pl.program_id(0)
    span = columns(step, LONG)
    srct_ref = all_src_ref.at[:, :, span]
    extra_ref = all_extra_ref.at[:, :, span]
    fov = lax.axis_index("fov")

    @pl.when(step == 0)
    def _():
        out_ref[...] = jnp.zeros_like(out_ref)
        pieces = []
        for k in range(5):
            mine = mine_ref[k]
            other = other_ref[k]
            pieces += [mine, other]
            first = jnp.where(fov == 0, mine, other)
            second = jnp.where(fov == 0, other, mine)
            for q in range(8):
                update_ref[k : k + 1, q * 256 : (q + 1) * 256] = first[q : q + 1]
                update_ref[k : k + 1, 2048 + q * 256 : 2048 + (q + 1) * 256] = second[q : q + 1]
        stacked = jnp.concatenate(pieces, axis=0)
        table_ref[...] = jnp.concatenate(split_parts(stacked, 3), axis=0)

    idx = idx_ref[0] ^ (fov * 2048)
    knot_sums = None
    slot_sums = None
    for part in range(LONG // CUT):
        cut = slice(part * CUT, (part + 1) * CUT)
        place = columns(step * (LONG // CUT) + part, CUT)
        high = rows_equal(16, idx[:, cut] >> 8)
        looked = dot_nn(table_ref[...], src_low_ref[:, place])
        looked = looked[:80] + looked[80:160] + looked[160:]
        chosen = [column_sum(looked[k * 16 : k * 16 + 16] * high) for k in range(5)]
        groups = []
        units = []
        for h in range(CUT // 128):
            lanes = slice(part * CUT + h * 128, part * CUT + (h + 1) * 128)
            spread = [jnp.broadcast_to(chosen[k][:, h * 128 : (h + 1) * 128], (8, 128)) for k in range(5)]
            sums = [None] * 17
            for o in range(OBS // 8):
                rows = slice(o * 8, o * 8 + 8)
                model = srct_ref[0, rows, lanes] * spread[0]
                for k in range(1, 5):
                    model = model + srct_ref[k, rows, lanes] * spread[k]
                residual = srct_ref[5, rows, lanes] - model
                phase = extra_ref[4, rows, lanes]
                moments = [extra_ref[c, rows, lanes] * residual for c in range(4)]
                terms = list(moments)
                for _ in range(3):
                    moments = [m * phase for m in moments]
                    terms += moments
                terms.append(extra_ref[5, rows, lanes] * residual)
                sums = terms if o == 0 else [s + t for s, t in zip(sums, terms)]
            groups.append(jnp.concatenate([fold(sums[:8]), fold(sums[8:16])], axis=0))
            units.append(column_sum(sums[16]))
        left = masked_rows(seg_high_ref[:, place], [jnp.concatenate(groups, axis=1)], 2)
        knot_part = repeated_dot(left, seg_low_ref[:, place], 2)
        left = masked_rows(place_ref[:, place], [jnp.concatenate(units, axis=1)], 2)
        slot_part = repeated_dot(left, owner_ref[:, place], 2)
        knot_sums = knot_part if part == 0 else knot_sums + knot_part
        slot_sums = slot_part if part == 0 else slot_sums + slot_part
    accumulate(acc_ref, knot_sums, step)
    accumulate(slot_ref, slot_sums, step)

    @pl.when(step == LONG_STEPS - 1)
    def _():
        tm = lax.axis_index("tm")
        slots = jnp.concatenate([slot_ref[...], slots_ref[...], jnp.zeros((CAP, RANGES), F32)], axis=0)
        out_ref[pl.ds(0, RANGES, stride=PIECES), :] = slots.T
        first_half = lax.broadcasted_iota(jnp.int32, (16, 128), 1) < 64
        for c in range(4):
            moments = [acc_ref[(k * 4 + c) * 16 : (k * 4 + c) * 16 + 16] for k in range(4)]
            right = knots_of([spline_from_moments(moments, j) for j in range(4)])
            far = pltpu.roll(diag_ref[c], 64, 1)
            start = tm * 2 * PIECES + 1 + c
            out_ref[pl.ds(start, 16, stride=8 * PIECES), :] = jnp.where(first_half, right, far)
            out_ref[pl.ds(start + PIECES, 16, stride=8 * PIECES), :] = jnp.where(first_half, far, right)


def attitude_kernel(in_ref, att_ref):
    base = lax.axis_index("tm") * 2 * PIECES + 1
    knots = None
    for s in range(16):
        for f in range(2):
            part = in_ref[pl.ds(base + (s * 8 + f) * PIECES, 4), :]
            knots = part if knots is None else knots + part
    lower = lax.broadcasted_iota(jnp.int32, (4, 128), 1) < 64
    mine = lower == (lax.axis_index("fov") == 0)
    att_ref[...] = jnp.where(mine, knots / (1.0 + pltpu.roll(knots, 64, 1)), 0.0)


def calibration_kernel(in_ref, cal_ref, left_ref, right_ref):
    slots = in_ref[pl.ds(0, RANGES, stride=PIECES), :].T
    unit = slots[64:96].astype(jnp.int32)
    parts = wide_parts(slots[:64], 2)
    for k in range(CAP):
        lanes = slice(k * 128, (k + 1) * 128)
        inner = unit[k : k + 1]
        right_ref[:, lanes] = narrow_rows_equal(128, inner & 127)
        high = narrow_rows_equal(32, inner >> 7)
        for n in range(2):
            for v in range(2):
                row = jnp.broadcast_to(parts[n][v * 32 + k : v * 32 + k + 1], (32, 128)).astype(BF16)
                left_ref[(n * 2 + v) * 32 : (n * 2 + v + 1) * 32, lanes] = high * row
    sums = dot_nt(left_ref[...], right_ref[...])
    sums = sums[:64] + sums[64:]
    cal_ref[...] = sums[:32] / (1.0 + sums[32:])


VMEM = pl.BlockSpec(memory_space=pltpu.VMEM)
SMEM = pl.BlockSpec(memory_space=pltpu.SMEM)
LONG_ROW = pl.BlockSpec((1, 1, LONG), lambda s: (s, 0, 0))
WIDE_ROW = pl.BlockSpec((1, 1, WIDE), lambda s: (s, 0, 0))


def on_chip(*arrays):
    return [pltpu.with_memory_space_constraint(a, pltpu.VMEM) for a in arrays]


def off_chip(*arrays):
    return [pltpu.with_memory_space_constraint(a, pltpu.HBM) for a in arrays]


def whole(shape):
    return pl.BlockSpec(shape, lambda s: (0,) * len(shape))


def shards(
    src_partials,
    att_partials,
    cal_partials,
    obs_phase,
    obs_residual,
    block_source,
    block_segment,
    block_unit,
    live_blocks,
):
    source = block_source.reshape(WIDE_STEPS, 1, WIDE)
    segment = block_segment.reshape(WIDE_STEPS, 1, WIDE)
    unit = block_unit.reshape(WIDE_STEPS, 1, WIDE)
    src = jnp.transpose(src_partials, (1, 0, 2))
    att = att_partials.reshape(BLK * 4, OBS)
    sequential = pltpu.CompilerParams(dimension_semantics=("arbitrary",), vmem_limit_bytes=24 * 1024 * 1024)
    small = pltpu.CompilerParams(vmem_limit_bytes=4 * 1024 * 1024)
    keep, send, srct, src_low = pl.pallas_call(
        normals_kernel,
        grid=(WIDE_STEPS,),
        in_specs=[
            SMEM,
            pl.BlockSpec((5, WIDE, OBS), lambda s: (0, s, 0)),
            pl.BlockSpec((WIDE, OBS), lambda s: (s, 0)),
            WIDE_ROW,
        ],
        out_specs=[VMEM] * 4,
        out_shape=[
            pltpu.VMEM((20, 8, 256), F32),
            pltpu.VMEM((20, 8, 256), F32),
            pltpu.VMEM((6, OBS, BLK), F32),
            pltpu.VMEM((256, BLK), BF16),
        ],
        scratch_shapes=[pltpu.VMEM((320, 256), F32)],
        compiler_params=sequential,
        name="normals",
    )(live_blocks, *off_chip(src, obs_residual, source))
    half = pl.pallas_call(
        join_kernel,
        in_specs=[VMEM] * 2,
        out_specs=VMEM,
        out_shape=pltpu.VMEM((20, 8, 256), F32),
        compiler_params=small,
        name="join",
    )(*on_chip(keep, lax.ppermute(send, "fov", [(0, 1), (1, 0)])))
    half, live_later = lax.optimization_barrier((half, live_blocks))
    around = [lax.ppermute(half, "tm", [(i, i ^ d) for i in range(4)]) for d in (1, 2, 3)]
    extra, seg_low, owner, seg_high, place, diag_knots, diag_slots = pl.pallas_call(
        diag_kernel,
        grid=(WIDE_STEPS,),
        in_specs=[
            SMEM,
            pl.BlockSpec((WIDE * 4, OBS), lambda s: (s, 0)),
            pl.BlockSpec((WIDE, OBS), lambda s: (s, 0)),
            pl.BlockSpec((WIDE, OBS), lambda s: (s, 0)),
            WIDE_ROW,
            WIDE_ROW,
        ],
        out_specs=[VMEM] * 7,
        out_shape=[
            pltpu.VMEM((6, OBS, BLK), F32),
            pltpu.VMEM((128, BLK), BF16),
            pltpu.VMEM((RANGES, BLK), BF16),
            pltpu.VMEM((16, BLK), BF16),
            pltpu.VMEM((CAP, BLK), BF16),
            pltpu.VMEM((4, 16, 128), F32),
            pltpu.VMEM((64, RANGES), F32),
        ],
        scratch_shapes=[
            pltpu.VMEM((256, 128), F32),
            pltpu.VMEM((64, RANGES), F32),
            pltpu.VMEM((RANGES, CUT), F32),
        ],
        compiler_params=sequential,
        cost_estimate=pl.CostEstimate(flops=200_000_000, bytes_accessed=12_000_000, transcendentals=0),
        name="diag",
    )(live_later, att, obs_phase, cal_partials, segment, unit)
    around, diag_knots = lax.optimization_barrier((around, diag_knots))
    mine = pl.pallas_call(
        solve_kernel,
        in_specs=[VMEM] * 4,
        out_specs=VMEM,
        out_shape=pltpu.VMEM((5, 8, 256), F32),
        compiler_params=small,
        name="solve",
    )(*on_chip(half, *around))
    other = lax.ppermute(mine, "fov", [(0, 1), (1, 0)])
    outgoing, src_update = pl.pallas_call(
        apply_kernel,
        grid=(LONG_STEPS,),
        in_specs=[VMEM] * 7 + [LONG_ROW] + [VMEM] * 4,
        out_specs=[VMEM, whole((5, 4096))],
        out_shape=[
            pltpu.VMEM((128 * PIECES, 128), F32),
            jax.ShapeDtypeStruct((5, 4096), F32),
        ],
        scratch_shapes=[
            pltpu.VMEM((240, 256), BF16),
            pltpu.VMEM((256, 128), F32),
            pltpu.VMEM((CAP, RANGES), F32),
        ],
        compiler_params=sequential,
        name="apply",
    )(
        *on_chip(srct, extra, src_low, seg_low, owner, seg_high, place),
        source.reshape(LONG_STEPS, 1, LONG),
        *on_chip(mine, other, diag_knots, diag_slots),
    )
    arrived = lax.all_to_all(
        outgoing.reshape(128, 1, PIECES * 128), ALL, split_axis=0, concat_axis=0, tiled=True
    ).reshape(128 * PIECES, 128)
    att_half = pl.pallas_call(
        attitude_kernel,
        in_specs=[VMEM],
        out_specs=VMEM,
        out_shape=pltpu.VMEM((4, 128), F32),
        compiler_params=small,
        name="attitude",
    )(*on_chip(arrived))
    att_other = lax.ppermute(att_half, "fov", [(0, 1), (1, 0)])
    cal_update = pl.pallas_call(
        calibration_kernel,
        in_specs=[VMEM],
        out_specs=VMEM,
        out_shape=jax.ShapeDtypeStruct((32, 128), F32),
        scratch_shapes=[pltpu.VMEM((128, CAP * 128), BF16), pltpu.VMEM((128, CAP * 128), BF16)],
        cost_estimate=pl.CostEstimate(flops=100_000_000, bytes_accessed=400_000, transcendentals=0),
        name="calibration",
    )(*on_chip(arrived))
    att_update = att_half + att_other
    return (src_update, att_update.reshape(4, 1, 128), cal_update.reshape(SHARE))


def solution(mesh):
    return jax.shard_map(
        shards,
        mesh=mesh,
        in_specs=(
            P(ALL, None, None),
            P(ALL, None, None),
            P(ALL, None),
            P(ALL, None),
            P(ALL, None),
            P(ALL),
            P(ALL),
            P(ALL),
            P(ALL),
        ),
        out_specs=(P(None, "sky"), P(None, "tm", "sky"), P(ALL)),
        check_vma=False,
    )
```
